768 devices in a mesh: ctx: 96 (over x, z_lo, y), tp: 8 (over z_hi, core).
Axes of the slice: x: 4, y: 8, z: 12 (z_hi: 4, z_lo: 3; z = z_hi * 3 + z_lo), core: 2. Of those that a mesh axis runs over, the one named last changes fastest.
Arguments:
- features: bfloat16 [3, 24576, 8192], P(None, 'ctx', 'tp'), may hold values from -6 to 6
- short_taps: bfloat16 [3, 512, 7], P(None, 'tp'), may hold values from -2 to 2
- long_taps: bfloat16 [512, 128], P('tp'), may hold values from -0.5 to 0.5
- skip_gain: bfloat16 [8192], P('tp'), may hold values from -4 to 4
- cotangent: bfloat16 [24576, 8192], P('ctx', 'tp'), may hold values from -6 to 6
Outputs:
- gated: bfloat16 [24576, 8192], P('ctx', 'tp')
- feature_grad: bfloat16 [3, 24576, 8192], P(None, 'ctx', 'tp')
- short_grad: float32 [3, 512, 7], P(None, 'tp')
- long_grad: float32 [512, 128], P('tp')
- skip_grad: float32 [8192], P('tp')
The draws below stay inside these ranges and needn't reach their ends.
All inputs are finite; a program needn't handle non-finite values.
Results may differ from the reference program's by a relative error of at most 0.0074.
Values may be sent and summed in bfloat16 or wider, within the bound.
No kernel may reach another device: no remote copies, remote signals or barrier semaphores. Data moves between devices by JAX's collectives and lax.ppermute only.
A program may use at most 128 MiB of HBM per device.

```python
import math
import jax
import jax.numpy as jnp
from jax import lax

D = 8192
SHORT = 7
LONG = 128
G = 512
TOKENS = 24576


def steps_of(own_key, extent, split, least, largest):
    level = 1.0
    for dim, parts in split:
        heights = jax.random.uniform(jax.random.fold_in(jax.random.fold_in(own_key, 6), dim), (parts,), jnp.float32, least / len(split), largest / len(split))
        level = level * jnp.repeat(jnp.exp(heights), extent[dim] // parts).reshape((-1,) + (1,) * (len(extent) - 1 - dim))
    return level


def scatter_about(rng, shape, scale, reach, cuts=(), held_as=jnp.bfloat16):
    factor_of = steps_of(rng, shape, cuts, -0.22, 0.18) if cuts else 1.0
    entries = jax.random.normal(rng, shape, jnp.float32) * scale * factor_of
    return jnp.minimum(jnp.maximum(entries, -reach), reach).astype(held_as)


def setup_inputs(seed: int = 0) -> dict:
    keys = jax.random.split(jax.random.key(seed), 6)
    return {
        "features": scatter_about(keys[0], (3, TOKENS, D), 1.0, 6.0, ((1, 96), (2, 8))),
        "short_taps": scatter_about(keys[1], (3, G, SHORT), SHORT ** -0.5, 2.0, ((1, 8),)),
        "long_taps": scatter_about(keys[2], (G, LONG), LONG ** -0.5, 0.5, ((0, 8),)),
        "skip_gain": scatter_about(keys[3], (D,), 1.0, 4.0, ((0, 8),)),
        "cotangent": scatter_about(keys[4], (TOKENS, D), 1.0, 6.0, ((0, 96), (1, 8))),
    }


def settle(values):
    return lax.optimization_barrier(values)

def causal_short(padded, taps, rows):
    total = jnp.zeros((rows,) + padded.shape[1:], jnp.float32)
    for offset in range(7):
        total = total + taps[:, :, offset] * padded[6 - offset:6 - offset + rows].astype(jnp.float32)
    return total

def block_pass(zblock, short_block, long_block, gain_block, grad_block):
    rows = zblock.shape[0]
    width = zblock.shape[2]
    taps = jnp.repeat(short_block, 16, axis=1).astype(jnp.float32)
    padded = jnp.concatenate([jnp.zeros((6, 3, width), zblock.dtype), zblock], axis=0)
    mixed = settle(causal_short(padded, taps, rows).astype(jnp.bfloat16))
    query = mixed[:, 0].astype(jnp.float32)
    key = mixed[:, 1].astype(jnp.float32)
    value = mixed[:, 2].astype(jnp.float32)
    product = settle((key * value).astype(jnp.bfloat16))
    prod_f = product.astype(jnp.float32)
    length = rows + 128
    filt = jnp.repeat(long_block, 16, axis=0).astype(jnp.float32).T
    spectrum = jnp.fft.rfft(filt, n=length, axis=0)
    prod_spec = jnp.fft.rfft(prod_f, n=length, axis=0)
    conv = jnp.fft.irfft(prod_spec * spectrum, n=length, axis=0)[:rows]
    gain = gain_block.astype(jnp.float32)
    inner = conv + gain * prod_f
    gated = (query * inner).astype(jnp.bfloat16)
    grad_in = grad_block.astype(jnp.float32)
    grad_query = grad_in * inner
    grad_inner = settle((grad_in * query).astype(jnp.bfloat16))
    inner_f = grad_inner.astype(jnp.float32)
    inner_spec = jnp.fft.rfft(inner_f, n=length, axis=0)
    back = jnp.fft.irfft(inner_spec * jnp.conj(spectrum), n=length, axis=0)[:rows]
    grad_product = settle((back + gain * inner_f).astype(jnp.bfloat16))
    product_g = grad_product.astype(jnp.float32)
    grad_mixed = settle(jnp.stack([grad_query, product_g * value, product_g * key], axis=1).astype(jnp.bfloat16))
    mixed_g = grad_mixed.astype(jnp.float32)
    trailing = jnp.concatenate([mixed_g, jnp.zeros((6, 3, width), jnp.float32)], axis=0)
    feature_grad = jnp.zeros((rows, 3, width), jnp.float32)
    for offset in range(7):
        feature_grad = feature_grad + taps[:, :, offset] * trailing[offset:offset + rows]
    feature_grad = feature_grad.astype(jnp.bfloat16)
    corr = jnp.fft.irfft(inner_spec * jnp.conj(prod_spec), n=length, axis=0)[:128]
    long_grad = corr.T.reshape(width // 16, 16, 128).sum(axis=1)
    skip_grad = lax.optimization_barrier(jnp.sum(inner_f * prod_f, axis=0))
    short_all = jnp.stack([lax.optimization_barrier(jnp.sum(mixed_g * padded[6 - offset:6 - offset + rows].astype(jnp.float32), axis=0)) for offset in range(7)], axis=-1)
    short_grad = short_all.reshape(3, width // 16, 16, 7).sum(axis=2)
    return (gated, feature_grad, short_grad, long_grad, skip_grad)

def reference(features, short_taps, long_taps, skip_gain, cotangent):
    block = min(D, 512)
    count = D // block
    init = (jnp.zeros((TOKENS, D), jnp.bfloat16), jnp.zeros((3, TOKENS, D), jnp.bfloat16), jnp.zeros((3, G, 7), jnp.float32), jnp.zeros((G, 128), jnp.float32), jnp.zeros((D,), jnp.float32))

    def step(index, carry):
        start = (index * block).astype(jnp.int32)
        gstart = (index * (block // 16)).astype(jnp.int32)
        zblock = jnp.transpose(lax.dynamic_slice_in_dim(features, start, block, 2), (1, 0, 2))
        short_block = lax.dynamic_slice_in_dim(short_taps, gstart, block // 16, 1)
        long_block = lax.dynamic_slice_in_dim(long_taps, gstart, block // 16, 0)
        gain_block = lax.dynamic_slice_in_dim(skip_gain, start, block, 0)
        grad_block = lax.dynamic_slice_in_dim(cotangent, start, block, 1)
        gated, feature_grad, short_grad, long_grad, skip_grad = block_pass(zblock, short_block, long_block, gain_block, grad_block)
        return (lax.dynamic_update_slice_in_dim(carry[0], gated, start, 1), lax.dynamic_update_slice_in_dim(carry[1], jnp.transpose(feature_grad, (1, 0, 2)), start, 2), lax.dynamic_update_slice_in_dim(carry[2], short_grad, gstart, 1), lax.dynamic_update_slice_in_dim(carry[3], long_grad, gstart, 0), lax.dynamic_update_slice_in_dim(carry[4], skip_grad, start, 0))
    gated, feature_grad, short_grad, long_grad, skip_grad = lax.fori_loop(0, count, step, init)
    group_scale = 1.0 / math.sqrt(16.0 * TOKENS)
    token_scale = 1.0 / math.sqrt(1.0 * TOKENS)
    return (gated, feature_grad, short_grad * group_scale, long_grad * group_scale, skip_grad * token_scale)
```

```python
import functools
import math

import jax
import jax.numpy as jnp
from jax import lax
from jax.experimental import pallas as pl
from jax.experimental.pallas import tpu as pltpu
from jax.sharding import Mesh
from jax.sharding import PartitionSpec as P

CTX = ("ctx_0", "ctx_1", "ctx_2")
SPLIT = (4, 3, 8)
LANES = 128
GROUPS = 8
STEP = 16
WINDOW = 144
BF16 = jnp.bfloat16
F32 = jnp.float32


def passed_along(block, axis, distance):
    devices = range(lax.axis_size(axis))
    route = [(i - distance, i) for i in devices if i - distance in devices]
    return lax.ppermute(block, axis, route)


def iota(shape, dim):
    return lax.broadcasted_iota(jnp.int32, shape, dim)


def channel_taps(taps_ref, out_ref, block):
    groups = taps_ref.shape[2]
    spread = iota((groups, LANES), 0) == GROUPS * block + iota((groups, LANES), 1) // 16
    spread = spread.astype(F32).astype(BF16)
    for i in range(3):
        out_ref[8 * i : 8 * i + 7, :] = jnp.dot(
            taps_ref[i], spread, preferred_element_type=F32
        )


def causal(ref, i, start, rows, taps):
    total = None
    for j in range(7):
        term = taps[8 * i + j : 8 * i + j + 1, :] * ref[i, start - j : start - j + rows, :]
        total = term if total is None else total + term
    return total.astype(BF16)


def edge_kernel(feat_ref, cot_ref, taps_ref, up_ref, down_ref, taps, raw):
    rows = feat_ref.shape[1]
    channel_taps(taps_ref, taps, pl.program_id(0))
    weights = taps[...]
    raw[0, 0:8, :] = jnp.zeros((8, LANES), F32)
    raw[0, 8:152, :] = feat_ref[0, 0:144, :].astype(F32)
    for i in (1, 2):
        raw[i, 0:144, :] = feat_ref[i, rows - 144 : rows, :].astype(F32)
    key = causal(raw, 1, 16, 128, weights).astype(F32)
    value = causal(raw, 2, 16, 128, weights).astype(F32)
    up_ref[0:128, :] = (key * value).astype(BF16)
    last = [feat_ref[i, rows - 16 : rows, :].astype(F32)[8:16] for i in range(3)]
    blank = jnp.zeros((8, LANES), F32)
    up_ref[128:160, :] = jnp.concatenate(last + [blank], axis=0).astype(BF16)
    query = causal(raw, 0, 8, 136, weights).astype(F32)
    grad = cot_ref[0:144, :].astype(F32)
    inner = grad[0:136] * query
    first = jnp.where(iota((8, LANES), 0) < 6, grad[0:8], inner[0:8])
    begin = [feat_ref[i, 0:16, :].astype(F32)[0:8] for i in range(3)]
    down_ref[...] = jnp.concatenate([first, inner[8:136]] + begin, axis=0).astype(BF16)


def local_kernel(
    feat_ref, cot_ref, taps_ref, long_ref,
    mixed_ref, product_ref, inner_ref, ahead_ref, behind_ref, taps_out, raw, filt, spread,
):
    step = pl.program_id(0)
    rows = feat_ref.shape[1]

    @pl.when(step == 0)
    def _():
        groups = long_ref.shape[0]
        flip = iota((128, 256), 0) + iota((128, 256), 1) == 128
        flip = flip.astype(F32).astype(BF16)
        filt[0] = jnp.dot(long_ref[...], flip, preferred_element_type=F32)
        filt[1, :, 0:128] = long_ref[...].astype(F32)
        filt[1, :, 128:256] = jnp.zeros((groups, 128), F32)

    taps_out[...] = jnp.zeros(taps_out.shape, F32)
    channel_taps(taps_ref, taps_out, step)
    weights = taps_out[...]
    for which, out in ((0, ahead_ref), (1, behind_ref)):
        base = filt[which, pl.ds(pl.multiple_of(GROUPS * step, GROUPS), GROUPS), :]
        for r in range(STEP):
            moved = base if r == 0 else pltpu.roll(base, r, 1)
            for half in (0, 1):
                lanes = moved[:, 128 * half : 128 * half + 128]
                spread[half, pl.ds(r, GROUPS, stride=STEP), :] = lanes
        for half in (0, 1):
            out[:, 128 * half : 128 * half + 128] = spread[half].astype(BF16)
    for i in range(3):
        raw[i, 0:8, :] = jnp.zeros((8, LANES), F32)
        raw[i, 8 : 8 + rows, :] = feat_ref[i].astype(F32)
    query, key, value = [causal(raw, i, 8, rows, weights) for i in range(3)]
    mixed_ref[0] = query
    mixed_ref[1] = key
    mixed_ref[2] = value
    product_ref[...] = (key.astype(F32) * value.astype(F32)).astype(BF16)
    inner_ref[...] = (cot_ref[...].astype(F32) * query.astype(F32)).astype(BF16)


def pick_groups(full, masks):
    total = full[0:STEP]
    for g in range(1, GROUPS):
        total = jnp.where(masks[g], full[STEP * g : STEP * g + STEP], total)
    return total


def main_kernel(
    feat_ref, cot_ref, gain_ref, mixed_ref, product_ref, inner_ref, ahead_ref, behind_ref, taps_ref,
    up_ref, down_ref,
    gated_ref, grad_ref, sums_ref,
    raw, mix, prod, ginn, gmix, cot, corr,
):
    step = pl.program_id(0)
    rows = feat_ref.shape[1]
    chunks = rows // STEP
    weights = taps_ref[...]
    gain = gain_ref[...].astype(F32)
    group_of = iota((STEP, LANES), 1) // 16
    masks = [group_of == g for g in range(GROUPS)]

    before = up_ref[128:160, :].astype(F32)
    tail = down_ref[128:160, :].astype(F32)
    for i in range(3):
        raw[i, 0:8, :] = before[8 * i : 8 * i + 8]
        raw[i, 8 : 8 + rows, :] = feat_ref[i].astype(F32)
        raw[i, 8 + rows : 16 + rows, :] = tail[8 + 8 * i : 16 + 8 * i]
    for i in range(3):
        mix[i, 8:rows, :] = mixed_ref[i].astype(F32)[8:rows]
        mix[i, 0:8, :] = causal(raw, i, 8, 8, weights).astype(F32)
        mix[i, rows : rows + 8, :] = causal(raw, i, 8 + rows, 8, weights).astype(F32)
        mix[i, rows + 8 : rows + 16, :] = jnp.zeros((8, LANES), F32)
    opening = down_ref[0:16, :].astype(F32)
    past = iota((STEP, LANES), 0) < 6
    after = jnp.where(past, opening, 0.0)
    cot[0:rows, :] = cot_ref[...].astype(F32)
    cot[rows : rows + 16, :] = after

    prod[0:128, :] = up_ref[0:128, :]
    prod[128 : 128 + rows, :] = product_ref[...]
    prod[128:144, :] = (mix[1, 0:16, :] * mix[2, 0:16, :]).astype(BF16)
    prod[128 + rows : 144 + rows, :] = (
        mix[1, rows : rows + 16, :] * mix[2, rows : rows + 16, :]
    ).astype(BF16)
    ginn[0:rows, :] = inner_ref[...]
    ginn[0:16, :] = (cot[0:16, :] * mix[0, 0:16, :]).astype(BF16)
    ginn[rows : rows + 128, :] = down_ref[0:128, :]
    ginn[rows : rows + 16, :] = jnp.where(
        past, after * mix[0, rows : rows + 16, :], opening
    ).astype(BF16)
    ginn[rows + 128 : rows + 144, :] = jnp.concatenate(
        [tail[0:8], jnp.zeros((8, LANES), F32)], axis=0
    ).astype(BF16)

    ahead = ahead_ref[:, 0:WINDOW]
    behind = behind_ref[:, 0:WINDOW]
    skip = jnp.zeros((STEP, LANES), F32)
    grid = jnp.zeros((LANES, WINDOW), F32)
    keep = [m.astype(F32).astype(BF16) for m in masks]
    for pair in range(0, chunks + 1, 2):
        own = [b for b in (pair, pair + 1) if b <= chunks]

        def windows(ref):
            parts = [ref[STEP * b : STEP * b + WINDOW, :] for b in own]
            return parts[0] if len(parts) == 1 else jnp.concatenate(parts, axis=1)

        forward = jnp.dot(ahead, windows(prod), preferred_element_type=F32)
        inn_windows = windows(ginn)
        backward = jnp.dot(behind, inn_windows, preferred_element_type=F32)
        if pair < chunks:
            pieces = [prod[128 + STEP * b : 144 + STEP * b, :] for b in own]
            left = jnp.concatenate(
                [jnp.concatenate([k * p for p in pieces], axis=1) for k in keep], axis=0
            )
            grid = grid + lax.dot_general(
                left, inn_windows, (((1,), (1,)), ((), ())), preferred_element_type=F32
            )
        for n, b in enumerate(own):
            lo, hi = STEP * b, STEP * b + STEP
            conv = pick_groups(forward[:, LANES * n : LANES * n + LANES], masks)
            back = pick_groups(backward[:, LANES * n : LANES * n + LANES], masks)
            p = prod[128 + lo : 128 + hi, :].astype(F32)
            q = ginn[lo:hi, :].astype(F32)
            inner = conv + gain * p
            gprod = (back + gain * q).astype(BF16).astype(F32)
            gmix[0, lo:hi, :] = (cot[lo:hi, :] * inner).astype(BF16).astype(F32)
            gmix[1, lo:hi, :] = (gprod * mix[2, lo:hi, :]).astype(BF16).astype(F32)
            gmix[2, lo:hi, :] = (gprod * mix[1, lo:hi, :]).astype(BF16).astype(F32)
            if b < chunks:
                gated_ref[lo:hi, :] = (mix[0, lo:hi, :] * inner).astype(BF16)
                skip = skip + p * q

    for i in range(3):
        total = None
        for j in range(7):
            term = weights[8 * i + j : 8 * i + j + 1, :] * gmix[i, j : j + rows, :]
            total = term if total is None else total + term
        grad_ref[i] = total.astype(BF16)

    lines = []
    for i in range(3):
        for j in range(7):
            both = gmix[i, 0:rows, :] * raw[i, 8 - j : 8 - j + rows, :]
            lines.append(jnp.sum(both, axis=0, keepdims=True))
        lines.append(jnp.zeros((1, LANES), F32))
    lines = jnp.concatenate(lines, axis=0)
    gather = iota((LANES, LANES), 1) == GROUPS * step + iota((LANES, LANES), 0) // 16
    gather = gather.astype(F32)
    short = jnp.dot(lines, gather, precision=lax.Precision.HIGHEST, preferred_element_type=F32)

    @pl.when(step == 0)
    def _():
        sums_ref[72:96, :] = short

    @pl.when(step > 0)
    def _():
        sums_ref[72:96, :] += short

    sums_ref[pl.ds(64 + step, 1), :] = jnp.sum(skip, axis=0, keepdims=True)
    corr[0] = grid[:, 0:128]
    corr[1, :, 0 : WINDOW - 128] = grid[:, 128:WINDOW]
    corr[1, :, WINDOW - 128 : 128] = jnp.zeros((LANES, 256 - WINDOW), F32)
    total = None
    for r in range(STEP):
        line = jnp.concatenate(
            [corr[half, pl.ds(r, GROUPS, stride=STEP), :] for half in (0, 1)], axis=1
        )
        line = line if r == 0 else pltpu.roll(line, 256 - r, 1)
        total = line[:, 0:128] if total is None else total + line[:, 0:128]
    sums_ref[pl.ds(pl.multiple_of(GROUPS * step, GROUPS), GROUPS), :] = total


def blocks3(rows):
    return pl.BlockSpec((3, rows, LANES), lambda b: (0, 0, b))


def blocks2(rows):
    return pl.BlockSpec((rows, LANES), lambda b: (0, b))


def whole(shape):
    return pl.BlockSpec(shape, lambda b: (0,) * len(shape))


def swap(values, axes):
    return lax.all_to_all(values, axes, 0, 0, tiled=True)


def summed(local):
    near, far = CTX[:2], CTX[2]
    parts = lax.axis_size(near)
    size = lax.axis_size(far)
    share = local.reshape(parts, -1, LANES)
    share = swap(share, near).sum(axis=0)
    every = jnp.broadcast_to(share[None], (size,) + share.shape)
    share = swap(every, far).sum(axis=0)
    every = jnp.broadcast_to(share[None], (parts,) + share.shape)
    return swap(every, near).reshape(local.shape)


def body(features, short_taps, long_taps, skip_gain, cotangent):
    rows, width = features.shape[1:]
    groups = width // 16
    steps = width // LANES
    shape = jax.ShapeDtypeStruct
    params = pltpu.CompilerParams(
        dimension_semantics=("arbitrary",), vmem_limit_bytes=16 * 2**20
    )
    short_taps = short_taps.transpose(0, 2, 1)
    up, down = pl.pallas_call(
        edge_kernel,
        grid=(steps,),
        in_specs=[blocks3(rows), blocks2(rows), whole((3, 7, groups))],
        out_specs=[blocks2(160), blocks2(160)],
        out_shape=[shape((160, width), BF16), shape((160, width), BF16)],
        scratch_shapes=[pltpu.VMEM((24, LANES), F32), pltpu.VMEM((3, 152, LANES), F32)],
        compiler_params=params,
        cost_estimate=pl.CostEstimate(flops=10**7, bytes_accessed=3 * 10**6, transcendentals=0),
        name="edge",
    )(features, cotangent, short_taps)
    from_last = passed_along(up, CTX, 1)
    from_next = passed_along(down, CTX, -1)
    mixed, product, inner, ahead, behind, taps = pl.pallas_call(
        local_kernel,
        grid=(steps,),
        in_specs=[
            blocks3(rows), blocks2(rows), whole((3, 7, groups)), whole((groups, 128)),
        ],
        out_specs=[
            blocks3(rows), blocks2(rows), blocks2(rows),
            pl.BlockSpec((128, 256), lambda b: (b, 0)),
            pl.BlockSpec((128, 256), lambda b: (b, 0)),
            blocks2(24),
        ],
        out_shape=[
            shape((3, rows, width), BF16), shape((rows, width), BF16), shape((rows, width), BF16),
            shape((groups * 16, 256), BF16), shape((groups * 16, 256), BF16),
            shape((24, width), F32),
        ],
        scratch_shapes=[
            pltpu.VMEM((3, rows + 8, LANES), F32),
            pltpu.VMEM((2, groups, 256), F32),
            pltpu.VMEM((2, 128, LANES), F32),
        ],
        compiler_params=params,
        cost_estimate=pl.CostEstimate(
            flops=2 * 10**7, bytes_accessed=8 * 10**6, transcendentals=0
        ),
        name="local",
    )(features, cotangent, short_taps, long_taps)
    gated, feature_grad, sums = pl.pallas_call(
        main_kernel,
        grid=(steps,),
        in_specs=[
            blocks3(rows), blocks2(rows), blocks2(1), blocks3(rows), blocks2(rows), blocks2(rows),
            pl.BlockSpec((128, 256), lambda b: (b, 0)),
            pl.BlockSpec((128, 256), lambda b: (b, 0)),
            blocks2(24), blocks2(160), blocks2(160),
        ],
        out_specs=[blocks2(rows), blocks3(rows), whole((96, LANES))],
        out_shape=[
            shape((rows, width), BF16), shape((3, rows, width), BF16), shape((96, LANES), F32),
        ],
        scratch_shapes=[
            pltpu.VMEM((3, rows + 16, LANES), F32),
            pltpu.VMEM((3, rows + 16, LANES), F32),
            pltpu.VMEM((rows + 144, LANES), BF16),
            pltpu.VMEM((rows + 144, LANES), BF16),
            pltpu.VMEM((3, rows + 16, LANES), F32),
            pltpu.VMEM((rows + 16, LANES), F32),
            pltpu.VMEM((2, 128, LANES), F32),
        ],
        compiler_params=params,
        cost_estimate=pl.CostEstimate(
            flops=10**8, bytes_accessed=10**7, transcendentals=0
        ),
        name="main",
    )(
        features, cotangent, skip_gain.reshape(1, width), mixed, product, inner, ahead, behind,
        taps, from_last, from_next,
    )
    total = summed(sums)
    tokens = rows * lax.axis_size(CTX)
    group_scale = 1.0 / math.sqrt(16.0 * tokens)
    token_scale = 1.0 / math.sqrt(1.0 * tokens)
    short = total[72:96].reshape(3, 8, LANES)[:, :7, :groups].transpose(0, 2, 1)
    return (
        gated,
        feature_grad,
        short * group_scale,
        total[:groups] * group_scale,
        total[64 : 64 + steps].reshape(width) * token_scale,
    )


def solution(mesh):
    torus = Mesh(mesh.devices.reshape(*SPLIT, mesh.shape["tp"]), CTX + ("tp",))
    return jax.shard_map(
        body,
        mesh=torus,
        in_specs=(P(None, CTX, "tp"), P(None, "tp", None), P("tp", None), P("tp"), P(CTX, "tp")),
        out_specs=(P(CTX, "tp"), P(None, CTX, "tp"), P(None, "tp", None), P("tp", None), P("tp")),
        check_vma=False,
    )
```

```python
import functools
import math

import jax
import jax.numpy as jnp
from jax import lax
from jax.experimental import pallas as pl
from jax.experimental.pallas import tpu as pltpu
from jax.sharding import Mesh
from jax.sharding import PartitionSpec as P

CTX = ("ctx_0", "ctx_1", "ctx_2")
SPLIT = (4, 3, 8)
LANES = 128
GROUPS = 8
STEP = 16
WINDOW = 144
BF16 = jnp.bfloat16
F32 = jnp.float32
SMALL = 4 * 2**20
WIDE, NARROW = 60 * 2**20, 56 * 2**20


def passed_along(block, axis, distance):
    devices = range(lax.axis_size(axis))
    route = [(i - distance, i) for i in devices if i - distance in devices]
    return lax.ppermute(block, axis, route)


def iota(shape, dim):
    return lax.broadcasted_iota(jnp.int32, shape, dim)


def channel_taps(taps_ref, out_ref, block):
    groups = taps_ref.shape[2]
    spread = iota((groups, LANES), 0) == GROUPS * block + iota((groups, LANES), 1) // 16
    spread = spread.astype(F32).astype(BF16)
    for i in range(3):
        out_ref[8 * i : 8 * i + 7, :] = jnp.dot(
            taps_ref[i], spread, preferred_element_type=F32
        )


def causal(ref, i, start, rows, taps):
    total = None
    for j in range(7):
        term = taps[8 * i + j : 8 * i + j + 1, :] * ref[i, start - j : start - j + rows, :]
        total = term if total is None else total + term
    return total.astype(BF16)


def edge_kernel(feat_ref, cot_ref, taps_ref, up_ref, down_ref, taps, raw):
    rows = feat_ref.shape[1]
    channel_taps(taps_ref, taps, pl.program_id(0))
    weights = taps[...]
    raw[0, 0:8, :] = jnp.zeros((8, LANES), F32)
    raw[0, 8:152, :] = feat_ref[0, 0:144, :].astype(F32)
    for i in (1, 2):
        raw[i, 0:144, :] = feat_ref[i, rows - 144 : rows, :].astype(F32)
    key = causal(raw, 1, 16, 128, weights).astype(F32)
    value = causal(raw, 2, 16, 128, weights).astype(F32)
    up_ref[0:128, :] = (key * value).astype(BF16)
    last = [feat_ref[i, rows - 16 : rows, :].astype(F32)[8:16] for i in range(3)]
    blank = jnp.zeros((8, LANES), F32)
    up_ref[128:160, :] = jnp.concatenate(last + [blank], axis=0).astype(BF16)
    query = causal(raw, 0, 8, 136, weights).astype(F32)
    grad = cot_ref[0:144, :].astype(F32)
    inner = grad[0:136] * query
    first = jnp.where(iota((8, LANES), 0) < 6, grad[0:8], inner[0:8])
    begin = [feat_ref[i, 0:16, :].astype(F32)[0:8] for i in range(3)]
    down_ref[...] = jnp.concatenate([first, inner[8:136]] + begin, axis=0).astype(BF16)


def pick_groups(full, masks):
    total = full[0:STEP]
    for g in range(1, GROUPS):
        total = jnp.where(masks[g], full[STEP * g : STEP * g + STEP], total)
    return total


def group_masks():
    group_of = iota((STEP, LANES), 1) // 16
    return [group_of == g for g in range(GROUPS)]


def filtered(matrix, ref, shift, chunks, masks):
    for at in range(0, len(chunks), 2):
        own = chunks[at : at + 2]
        parts = [ref[STEP * b + shift : STEP * b + shift + WINDOW, :] for b in own]
        parts = parts[0] if len(parts) == 1 else jnp.concatenate(parts, axis=1)
        full = jnp.dot(matrix, parts, preferred_element_type=F32)
        for n, b in enumerate(own):
            yield b, pick_groups(full[:, LANES * n : LANES * n + LANES], masks)


def inside(rows):
    chunks = rows // STEP
    return list(range(9, chunks)), list(range(1, chunks - 8))


def local_kernel(
    feat_ref, cot_ref, taps_ref, long_ref, gain_ref,
    mixed_ref, product_ref, inner_ref, ahead_ref, behind_ref, taps_out, conv_ref, back_ref,
    raw, filt, spread,
):
    step = pl.program_id(0)
    rows = feat_ref.shape[1]

    @pl.when(step == 0)
    def _():
        groups = long_ref.shape[0]
        flip = iota((128, 256), 0) + iota((128, 256), 1) == 128
        flip = flip.astype(F32).astype(BF16)
        filt[0] = jnp.dot(long_ref[...], flip, preferred_element_type=F32)
        filt[1, :, 0:128] = long_ref[...].astype(F32)
        filt[1, :, 128:256] = jnp.zeros((groups, 128), F32)

    taps_out[...] = jnp.zeros(taps_out.shape, F32)
    channel_taps(taps_ref, taps_out, step)
    taps_out[7:8, :] = gain_ref[...].astype(F32)
    weights = taps_out[...]
    for which, out in ((0, ahead_ref), (1, behind_ref)):
        base = filt[which, pl.ds(pl.multiple_of(GROUPS * step, GROUPS), GROUPS), :]
        for r in range(STEP):
            moved = base if r == 0 else pltpu.roll(base, r, 1)
            for half in (0, 1):
                lanes = moved[:, 128 * half : 128 * half + 128]
                spread[which, half, pl.ds(r, GROUPS, stride=STEP), :] = lanes
        for half in (0, 1):
            out[:, 128 * half : 128 * half + 128] = spread[which, half].astype(BF16)
    for i in range(3):
        raw[i, 0:8, :] = jnp.zeros((8, LANES), F32)
        raw[i, 8 : 8 + rows, :] = feat_ref[i].astype(F32)
    size = 64
    for lo in range(0, rows, size):
        query, key, value = [causal(raw, i, 8 + lo, size, weights) for i in range(3)]
        mixed_ref[0, lo : lo + size, :] = query
        mixed_ref[1, lo : lo + size, :] = key
        mixed_ref[2, lo : lo + size, :] = value
        product_ref[lo : lo + size, :] = (key.astype(F32) * value.astype(F32)).astype(BF16)
        grad = cot_ref[lo : lo + size, :].astype(F32)
        inner_ref[lo : lo + size, :] = (grad * query.astype(F32)).astype(BF16)
    masks = group_masks()
    convs, backs = inside(rows)
    for b, conv in filtered(ahead_ref[:, 0:WINDOW], product_ref, -128, convs, masks):
        conv_ref[STEP * (b - convs[0]) : STEP * (b - convs[0]) + STEP, :] = conv
    for b, back in filtered(behind_ref[:, 0:WINDOW], inner_ref, 0, backs, masks):
        back_ref[STEP * (b - backs[0]) : STEP * (b - backs[0]) + STEP, :] = back


def corr_kernel(
    feat_ref, cot_ref, mixed_ref, product_ref, inner_ref, taps_ref, up_ref, down_ref,
    prod, ginn, edges_ref, sums_ref, raw, corr,
):
    rows = feat_ref.shape[1]
    chunks = rows // STEP
    weights = taps_ref[...]
    masks = group_masks()
    before = up_ref[128:160, :].astype(F32)
    tail = down_ref[128:160, :].astype(F32)
    start, end = [], []
    for i in range(3):
        raw[i, 0:8, :] = before[8 * i : 8 * i + 8]
        raw[i, 8:24, :] = feat_ref[i, 0:16, :].astype(F32)
        raw[i, 24:40, :] = feat_ref[i, rows - 16 : rows, :].astype(F32)
        raw[i, 40:48, :] = tail[8 + 8 * i : 16 + 8 * i]
        first = causal(raw, i, 8, 8, weights).astype(F32)
        start.append(jnp.concatenate([first, mixed_ref[i, 0:16, :].astype(F32)[8:16]], axis=0))
        past_end = causal(raw, i, 40, 8, weights).astype(F32)
        end.append(jnp.concatenate([past_end, jnp.zeros((8, LANES), F32)], axis=0))
        edges_ref[i, 0:16, :] = start[i].astype(BF16)
        edges_ref[i, 16:32, :] = end[i].astype(BF16)
    opening = down_ref[0:16, :].astype(F32)
    past = iota((STEP, LANES), 0) < 6
    after = jnp.where(past, opening, 0.0)
    edges_ref[3, 0:16, :] = cot_ref[0:16, :]
    edges_ref[3, 16:32, :] = after.astype(BF16)

    prod[0:128, :] = up_ref[0:128, :]
    prod[128:144, :] = (start[1] * start[2]).astype(BF16)
    prod[144 : 128 + rows, :] = product_ref[16:rows, :]
    prod[128 + rows : 144 + rows, :] = (end[1] * end[2]).astype(BF16)
    ginn[0:16, :] = (cot_ref[0:16, :].astype(F32) * start[0]).astype(BF16)
    ginn[16:rows, :] = inner_ref[16:rows, :]
    ginn[rows : rows + 16, :] = jnp.where(past, after * end[0], opening).astype(BF16)
    ginn[rows + 16 : rows + 128, :] = down_ref[16:128, :]
    ginn[rows + 128 : rows + 144, :] = jnp.concatenate(
        [tail[0:8], jnp.zeros((8, LANES), F32)], axis=0
    ).astype(BF16)

    skip = jnp.zeros((STEP, LANES), F32)
    grid = jnp.zeros((LANES, WINDOW), F32)
    keep = [m.astype(F32).astype(BF16) for m in masks]
    for pair in range(0, chunks, 2):
        lo = STEP * pair
        pieces = [prod[128 + lo : 144 + lo, :], prod[144 + lo : 160 + lo, :]]
        right = jnp.concatenate(
            [ginn[lo : lo + WINDOW, :], ginn[lo + STEP : lo + STEP + WINDOW, :]], axis=1
        )
        left = jnp.concatenate(
            [jnp.concatenate([k * p for p in pieces], axis=1) for k in keep], axis=0
        )
        grid = grid + lax.dot_general(
            left, right, (((1,), (1,)), ((), ())), preferred_element_type=F32
        )
        for n, piece in enumerate(pieces):
            at = lo + STEP * n
            skip = skip + piece.astype(F32) * ginn[at : at + STEP, :].astype(F32)
    corr[0] = grid[:, 0:128]
    corr[1, :, 0 : WINDOW - 128] = grid[:, 128:WINDOW]
    corr[1, :, WINDOW - 128 : 128] = jnp.zeros((LANES, 256 - WINDOW), F32)
    total = None
    for r in range(STEP):
        line = jnp.concatenate(
            [corr[half, pl.ds(r, GROUPS, stride=STEP), :] for half in (0, 1)], axis=1
        )
        line = line if r == 0 else pltpu.roll(line, 256 - r, 1)
        total = line[:, 0:128] if total is None else total + line[:, 0:128]
    sums_ref[0, 0:8, :] = total
    sums_ref[0, 8:16, :] = jnp.broadcast_to(jnp.sum(skip, axis=0, keepdims=True), (8, LANES))


def main_kernel(
    feat_ref, cot_ref, taps_ref, mixed_ref, prod, ginn, edges_ref, ahead_ref, behind_ref,
    conv_ref, back_ref,
    gated_ref, gmix_ref, short_ref,
    gmix,
):
    step = pl.program_id(0)
    rows = feat_ref.shape[1]
    chunks = rows // STEP
    gain = taps_ref[7:8, :]
    masks = group_masks()

    def mixed(i, b):
        if b == 0 or b == chunks:
            return edges_ref[i, STEP * (b > 0) : STEP * (b > 0) + STEP, :].astype(F32)
        if i == 3:
            return cot_ref[STEP * b : STEP * b + STEP, :].astype(F32)
        return mixed_ref[i, STEP * b : STEP * b + STEP, :].astype(F32)

    def keep(i, b, values):
        values = values.astype(BF16)
        gmix_ref[i, STEP * b : STEP * b + STEP, :] = values
        gmix[i, STEP * b : STEP * b + STEP, :] = values.astype(F32)

    def with_conv(b, conv):
        inner = conv + gain * prod[128 + STEP * b : 144 + STEP * b, :].astype(F32)
        keep(0, b, mixed(3, b) * inner)
        if b < chunks:
            gated_ref[STEP * b : STEP * b + STEP, :] = (mixed(0, b) * inner).astype(BF16)

    def with_back(b, back):
        grad = back + gain * ginn[STEP * b : STEP * b + STEP, :].astype(F32)
        grad = grad.astype(BF16).astype(F32)
        keep(1, b, grad * mixed(2, b))
        keep(2, b, grad * mixed(1, b))

    convs, backs = inside(rows)
    everything = range(chunks + 1)
    outer = [b for b in everything if b not in convs]
    for b, conv in filtered(ahead_ref[:, 0:WINDOW], prod, 0, outer, masks):
        with_conv(b, conv)
    for b in convs:
        with_conv(b, conv_ref[STEP * (b - convs[0]) : STEP * (b - convs[0]) + STEP, :])
    outer = [b for b in everything if b not in backs]
    for b, back in filtered(behind_ref[:, 0:WINDOW], ginn, 0, outer, masks):
        with_back(b, back)
    for b in backs:
        with_back(b, back_ref[STEP * (b - backs[0]) : STEP * (b - backs[0]) + STEP, :])

    size = 64
    lines = []
    for i in range(3):
        totals = [None] * 7
        for lo in range(0, rows, size):
            own = feat_ref[i, lo : lo + size, :].astype(F32)
            for j in range(7):
                both = gmix[i, lo + j : lo + j + size, :] * own
                both = both.reshape(size // 8, 8, LANES).sum(axis=0)
                totals[j] = both if totals[j] is None else totals[j] + both
        lines += [jnp.sum(total, axis=0, keepdims=True) for total in totals]
        lines.append(jnp.zeros((1, LANES), F32))
    group = GROUPS * step + iota((LANES, LANES), 0) // 16
    lane = iota((LANES, LANES), 1)
    short = None
    for part, shift in ((lines[0:16], 0), (lines[16:24] + [jnp.zeros((8, LANES), F32)], 64)):
        gather = (lane == group + shift).astype(F32)
        term = jnp.dot(
            jnp.concatenate(part, axis=0), gather,
            precision=lax.Precision.HIGHEST, preferred_element_type=F32,
        )
        short = term if short is None else short + term

    @pl.when(step == 0)
    def _():
        short_ref[...] = short

    @pl.when(step > 0)
    def _():
        short_ref[...] += short


def feature_kernel(gmix_ref, taps_ref, out_ref, wide):
    rows = out_ref.shape[1]
    weights = taps_ref[...]
    size = 64
    for i in range(3):
        wide[i] = gmix_ref[i].astype(F32)
    for i in range(3):
        for lo in range(0, rows, size):
            total = None
            for j in range(7):
                term = weights[8 * i + j : 8 * i + j + 1, :] * wide[i, lo + j : lo + j + size, :]
                total = term if total is None else total + term
            out_ref[i, lo : lo + size, :] = total.astype(BF16)


def join_kernel(long_ref, short_ref, out_ref):
    share = jnp.sum(long_ref[...], axis=0)
    long, skip = share[0:8], share[8:16]
    row = iota((8, LANES), 0)
    upper = iota((8, LANES), 1) >= 64
    swapped = pltpu.roll(skip, 64, 1)
    skip = jnp.where(row == 0, swapped, skip)
    low = jnp.where(upper & (row < 2), skip, short_ref[8:16, :])
    for n in range(out_ref.shape[0]):
        out_ref[n, 0:8, :] = short_ref[0:8, :]
        out_ref[n, 8:16, :] = low
        out_ref[n, 16:24, :] = long


def spread_kernel(in_ref, out_ref):
    total = jnp.sum(in_ref[...], axis=0)
    for n in range(out_ref.shape[0]):
        out_ref[n] = total


def final_kernel(group_scale, token_scale, in_ref, short_ref, long_ref, skip_ref):
    values = in_ref[...]
    sent = values.shape[0]
    short = jnp.sum(values[:, 0:16, :], axis=0)
    groups = short_ref.shape[2]
    moved = pltpu.roll(short, 64, 1)
    short_ref[0] = short[0:7, 0:groups] * group_scale
    short_ref[1] = short[8:15, 0:groups] * group_scale
    short_ref[2] = moved[0:7, 0:groups] * group_scale
    upper = iota((1, LANES), 1) >= 64
    for n in range(sent):
        long_ref[8 * n : 8 * n + 8, :] = values[n, 16:24, :] * group_scale
        pair = values[n, 8:16, :]
        turned = pltpu.roll(pair, 64, 1)
        skip_ref[n : n + 1, :] = jnp.where(upper, pair[1:2], turned[0:1]) * token_scale


def blocks3(rows):
    return pl.BlockSpec((3, rows, LANES), lambda b: (0, 0, b))


def blocks2(rows):
    return pl.BlockSpec((rows, LANES), lambda b: (0, b))


def whole(shape):
    return pl.BlockSpec(shape, lambda b: (0,) * len(shape))


def swap(values, axes):
    return lax.all_to_all(values, axes, 0, 0, tiled=True)


def body(features, short_taps, long_taps, skip_gain, cotangent):
    rows, width = features.shape[1:]
    groups = width // 16
    steps = width // LANES
    near, far = CTX[:2], CTX[2]
    shape = jax.ShapeDtypeStruct
    short_taps = short_taps.transpose(0, 2, 1)

    def call(kernel, name, ins, outs, scratch, bytes_accessed, limit=WIDE, grid=(steps,)):
        return pl.pallas_call(
            kernel,
            grid=grid,
            in_specs=ins,
            out_specs=[spec for spec, _ in outs],
            out_shape=[out for _, out in outs],
            scratch_shapes=scratch,
            compiler_params=pltpu.CompilerParams(
                dimension_semantics=("arbitrary",) * len(grid), vmem_limit_bytes=limit
            ),
            cost_estimate=pl.CostEstimate(
                flops=bytes_accessed, bytes_accessed=bytes_accessed, transcendentals=0
            ),
            name=name,
        )

    up, down = call(
        edge_kernel,
        "edge",
        [blocks3(rows), blocks2(rows), whole((3, 7, groups))],
        [
            (blocks2(160), shape((160, width), BF16)),
            (blocks2(160), shape((160, width), BF16)),
        ],
        [pltpu.VMEM((24, LANES), F32), pltpu.VMEM((3, 152, LANES), F32)],
        5 * 10**6,
    )(features, cotangent, short_taps)
    from_last = passed_along(up, CTX, 1)
    from_next = passed_along(down, CTX, -1)
    matrix = pl.BlockSpec((128, 256), lambda b: (b, 0))
    convs, backs = inside(rows)
    near_conv, near_back = STEP * len(convs), STEP * len(backs)
    mixed, product, inner, ahead, behind, taps, conv, back = call(
        local_kernel,
        "local",
        [
            blocks3(rows), blocks2(rows), whole((3, 7, groups)), whole((groups, 128)), blocks2(1),
        ],
        [
            (blocks3(rows), shape((3, rows, width), BF16)),
            (blocks2(rows), shape((rows, width), BF16)),
            (blocks2(rows), shape((rows, width), BF16)),
            (matrix, shape((groups * 16, 256), BF16)),
            (matrix, shape((groups * 16, 256), BF16)),
            (blocks2(24), shape((24, width), F32)),
            (blocks2(near_conv), shape((near_conv, width), F32)),
            (blocks2(near_back), shape((near_back, width), F32)),
        ],
        [
            pltpu.VMEM((3, rows + 8, LANES), F32),
            pltpu.VMEM((2, groups, 256), F32),
            pltpu.VMEM((2, 2, 128, LANES), F32),
        ],
        2 * 10**7,
    )(features, cotangent, short_taps, long_taps, skip_gain.reshape(1, width))
    prod, ginn, edges, sums = call(
        corr_kernel,
        "corr",
        [
            blocks3(rows), blocks2(rows), blocks3(rows), blocks2(rows), blocks2(rows), blocks2(24),
            blocks2(160), blocks2(160),
        ],
        [
            (blocks2(rows + 144), shape((rows + 144, width), BF16)),
            (blocks2(rows + 144), shape((rows + 144, width), BF16)),
            (pl.BlockSpec((4, 32, LANES), lambda b: (0, 0, b)), shape((4, 32, width), BF16)),
            (pl.BlockSpec((1, 16, LANES), lambda b: (b, 0, 0)), shape((steps, 16, LANES), F32)),
        ],
        [pltpu.VMEM((3, 48, LANES), F32), pltpu.VMEM((2, 128, LANES), F32)],
        10**7,
        NARROW,
    )(features, cotangent, mixed, product, inner, taps, from_last, from_next)
    sums = swap(sums, far)
    gated, gmix, short = call(
        main_kernel,
        "main",
        [
            blocks3(rows), blocks2(rows), blocks2(24), blocks3(rows), blocks2(rows + 144),
            blocks2(rows + 144), pl.BlockSpec((4, 32, LANES), lambda b: (0, 0, b)), matrix, matrix,
            blocks2(near_conv), blocks2(near_back),
        ],
        [
            (blocks2(rows), shape((rows, width), BF16)),
            (blocks3(rows + 16), shape((3, rows + 16, width), BF16)),
            (whole((16, LANES)), shape((16, LANES), F32)),
        ],
        [pltpu.VMEM((3, rows + 16, LANES), F32)],
        2 * 10**7,
    )(
        features, cotangent, taps, mixed, prod, ginn, edges, ahead, behind, conv, back,
    )
    parts = lax.axis_size(near)
    size = lax.axis_size(far)
    (joined,) = call(
        join_kernel,
        "join",
        [whole((size, 16, LANES)), whole((16, LANES))],
        [(whole((parts, 24, LANES)), shape((parts, 24, LANES), F32))],
        [],
        10**5,
        SMALL,
        grid=(1,),
    )(sums, short)
    joined = swap(joined, near)
    (feature_grad,) = call(
        feature_kernel,
        "features",
        [blocks3(rows + 16), blocks2(24)],
        [(blocks3(rows), shape((3, rows, width), BF16))],
        [pltpu.VMEM((3, rows + 16, LANES), F32)],
        10**7,
    )(gmix, taps)
    (every,) = call(
        spread_kernel,
        "spread",
        [whole((parts, 24, LANES))],
        [(whole((size, 24, LANES)), shape((size, 24, LANES), F32))],
        [],
        10**5,
        SMALL,
        grid=(1,),
    )(joined)
    every = swap(every, far)
    tokens = rows * lax.axis_size(CTX)
    group_scale = 1.0 / math.sqrt(16.0 * tokens)
    token_scale = 1.0 / math.sqrt(1.0 * tokens)
    short, long, skip = call(
        functools.partial(final_kernel, group_scale, token_scale),
        "final",
        [whole((size, 24, LANES))],
        [
            (whole((3, 7, groups)), shape((3, 7, groups), F32)),
            (whole((groups, LANES)), shape((groups, LANES), F32)),
            (whole((steps, LANES)), shape((steps, LANES), F32)),
        ],
        [],
        10**5,
        SMALL,
        grid=(1,),
    )(every)
    return gated, feature_grad, short.transpose(0, 2, 1), long, skip.reshape(width)


def solution(mesh):
    torus = Mesh(mesh.devices.reshape(*SPLIT, mesh.shape["tp"]), CTX + ("tp",))
    return jax.shard_map(
        body,
        mesh=torus,
        in_specs=(P(None, CTX, "tp"), P(None, "tp", None), P("tp", None), P("tp"), P(CTX, "tp")),
        out_specs=(P(CTX, "tp"), P(None, CTX, "tp"), P(None, "tp", None), P("tp", None), P("tp")),
        check_vma=False,
    )
```

```python
import functools
import math

import jax
import jax.numpy as jnp
from jax import lax
from jax.experimental import pallas as pl
from jax.experimental.pallas import tpu as pltpu
from jax.sharding import Mesh
from jax.sharding import PartitionSpec as P

CTX = ("ctx_0", "ctx_1", "ctx_2")
SPLIT = (4, 3, 8)
LANES = 128
GROUPS = 8
STEP = 16
WINDOW = 144
BF16 = jnp.bfloat16
F32 = jnp.float32
LIMIT = 16 * 2**20
EDGE_LIMIT = 60000 * 2**10


def passed_along(block, axis, distance):
    devices = range(lax.axis_size(axis))
    route = [(i - distance, i) for i in devices if i - distance in devices]
    return lax.ppermute(block, axis, route)


def iota(shape, dim):
    return lax.broadcasted_iota(jnp.int32, shape, dim)


def lanes_of(step):
    return pl.ds(pl.multiple_of(LANES * step, LANES), LANES)


def channel_taps(taps_ref, out_ref, block):
    groups = taps_ref.shape[2]
    spread = iota((groups, LANES), 0) == GROUPS * block + iota((groups, LANES), 1) // 16
    spread = spread.astype(F32).astype(BF16)
    for i in range(3):
        out_ref[8 * i : 8 * i + 7, :] = jnp.dot(
            taps_ref[i], spread, preferred_element_type=F32
        )


def causal(ref, i, start, rows, taps):
    total = None
    for j in range(7):
        term = taps[8 * i + j : 8 * i + j + 1, :] * ref[i, start - j : start - j + rows, :]
        total = term if total is None else total + term
    return total.astype(BF16)


def pick_groups(full, masks):
    total = full[0:STEP]
    for g in range(1, GROUPS):
        total = jnp.where(masks[g], full[STEP * g : STEP * g + STEP], total)
    return total


def group_masks():
    group_of = iota((STEP, LANES), 1) // 16
    return [group_of == g for g in range(GROUPS)]


def filtered(matrix, ref, shift, chunks, masks, lanes):
    for at in range(0, len(chunks), 2):
        own = chunks[at : at + 2]
        parts = [ref[STEP * b + shift : STEP * b + shift + WINDOW, lanes] for b in own]
        parts = parts[0] if len(parts) == 1 else jnp.concatenate(parts, axis=1)
        full = jnp.dot(matrix, parts, preferred_element_type=F32)
        for n, b in enumerate(own):
            yield b, pick_groups(full[:, LANES * n : LANES * n + LANES], masks)


def inside(rows):
    chunks = rows // STEP
    return list(range(9, chunks)), list(range(1, chunks - 8))


def correlated(grid, products, inners, chunks, keep):
    for at in range(0, len(chunks), 2):
        own = chunks[at : at + 2]
        pieces = [products(b) for b in own]
        windows = [inners(b) for b in own]
        right = windows[0] if len(own) == 1 else jnp.concatenate(windows, axis=1)
        left = []
        for k in keep:
            masked = [k * p for p in pieces]
            left.append(masked[0] if len(own) == 1 else jnp.concatenate(masked, axis=1))
        term = lax.dot_general(
            jnp.concatenate(left, axis=0), right, (((1,), (1,)), ((), ())),
            preferred_element_type=F32,
        )
        grid = term if grid is None else grid + term
    return grid


def short_pass(gmix, i, own, weights, totals, lo, size):
    grad = None
    for j in range(7):
        moved = gmix[i, lo + j : lo + j + size, :]
        term = weights[8 * i + j : 8 * i + j + 1, :] * moved
        grad = term if grad is None else grad + term
        both = (moved * own).reshape(size // 8, 8, LANES).sum(axis=0)
        totals[j] = both if totals[j] is None else totals[j] + both
    return grad.astype(BF16)


def settled(rows):
    return [rows - 112, 16, 16]


def edge_kernel(
    feat_hbm, cot_hbm, taps_hbm, up_ref, down_ref, taps, opens, closes, cot_ref, taps_ref, raw, sems,
):
    rows = cot_hbm.shape[0]
    pairs = [
        (taps_hbm, taps_ref),
        (feat_hbm.at[1, rows - 144 : rows], closes.at[1]),
        (feat_hbm.at[2, rows - 144 : rows], closes.at[2]),
        (feat_hbm.at[0, 0:144], opens.at[0]),
        (cot_hbm.at[0:144], cot_ref),
        (feat_hbm.at[0, rows - 16 : rows], closes.at[0, 128:144]),
        (feat_hbm.at[1, 0:16], opens.at[1, 0:16]),
        (feat_hbm.at[2, 0:16], opens.at[2, 0:16]),
    ]
    copies = [
        pltpu.make_async_copy(source, target, sems.at[n])
        for n, (source, target) in enumerate(pairs)
    ]
    for copy in copies:
        copy.start()
    for copy in copies:
        copy.wait()

    @pl.loop(0, cot_ref.shape[1] // LANES)
    def _(step):
        lanes = lanes_of(step)
        channel_taps(taps_ref, taps.at[:, lanes], step)
        weights = taps[:, lanes]
        raw[0, 0:8, :] = jnp.zeros((8, LANES), F32)
        raw[0, 8:152, :] = opens[0, :, lanes].astype(F32)
        for i in (1, 2):
            raw[i, 0:144, :] = closes[i, :, lanes].astype(F32)
        for lo in (0, 64):
            key = causal(raw, 1, 16 + lo, 64, weights).astype(F32)
            value = causal(raw, 2, 16 + lo, 64, weights).astype(F32)
            up_ref[lo : lo + 64, lanes] = (key * value).astype(BF16)
        last = [closes[i, 128:144, lanes].astype(F32)[8:16] for i in range(3)]
        blank = jnp.zeros((8, LANES), F32)
        up_ref[128:160, lanes] = jnp.concatenate(last + [blank], axis=0).astype(BF16)
        for lo in (0, 64):
            inner = causal(raw, 0, 8 + lo, 64, weights).astype(F32)
            grad = cot_ref[lo : lo + 64, lanes].astype(F32)
            inner = grad * inner
            if lo == 0:
                first = jnp.where(iota((8, LANES), 0) < 6, grad[0:8], inner[0:8])
                inner = jnp.concatenate([first, inner[8:64]], axis=0)
            down_ref[lo : lo + 64, lanes] = inner.astype(BF16)
        query = causal(raw, 0, 136, 8, weights).astype(F32)
        rest = cot_ref[128:144, lanes].astype(F32)[0:8] * query
        begin = [opens[i, 0:16, lanes].astype(F32)[0:8] for i in range(3)]
        down_ref[128:160, lanes] = jnp.concatenate([rest] + begin, axis=0).astype(BF16)


def local_kernel(
    feat_ref, cot_ref, taps_ref, long_ref, gain_ref,
    mixed_ref, product_ref, inner_ref, ahead_ref, behind_ref,
    gated_ref, grad_ref, gmix_ref, lines_ref, grid_ref,
    raw, filt, spread, gmix,
):
    rows = cot_ref.shape[0]
    groups = long_ref.shape[0]
    flip = iota((128, 256), 0) + iota((128, 256), 1) == 128
    flip = flip.astype(F32).astype(BF16)
    filt[0] = jnp.dot(long_ref[...], flip, preferred_element_type=F32)
    filt[1, :, 0:128] = long_ref[...].astype(F32)
    filt[1, :, 128:256] = jnp.zeros((groups, 128), F32)

    @pl.loop(0, cot_ref.shape[1] // LANES)
    def _(step):
        lanes = lanes_of(step)
        block = pl.ds(pl.multiple_of(LANES * step, LANES), LANES)
        gain = gain_ref[:, lanes].astype(F32)
        weights = taps_ref[:, lanes]
        for which, out in ((0, ahead_ref), (1, behind_ref)):
            base = filt[which, pl.ds(pl.multiple_of(GROUPS * step, GROUPS), GROUPS), :]
            for r in range(STEP):
                moved = base if r == 0 else pltpu.roll(base, r, 1)
                for half in (0, 1):
                    part = moved[:, 128 * half : 128 * half + 128]
                    spread[which, half, pl.ds(r, GROUPS, stride=STEP), :] = part
            for half in (0, 1):
                out[block, 128 * half : 128 * half + 128] = spread[which, half].astype(BF16)
        for i in range(3):
            raw[i, 0:8, :] = jnp.zeros((8, LANES), F32)
            raw[i, 8 : 8 + rows, :] = feat_ref[i, :, lanes].astype(F32)
        size = 64
        for lo in range(0, rows, size):
            query, key, value = [causal(raw, i, 8 + lo, size, weights) for i in range(3)]
            mixed_ref[0, lo : lo + size, lanes] = query
            mixed_ref[1, lo : lo + size, lanes] = key
            mixed_ref[2, lo : lo + size, lanes] = value
            both = key.astype(F32) * value.astype(F32)
            product_ref[lo : lo + size, lanes] = both.astype(BF16)
            grad = cot_ref[lo : lo + size, lanes].astype(F32)
            inner_ref[lo : lo + size, lanes] = (grad * query.astype(F32)).astype(BF16)
        masks = group_masks()
        keep = [m.astype(F32).astype(BF16) for m in masks]
        convs, backs = inside(rows)
        starts = settled(rows)
        matrix = ahead_ref[block, 0:WINDOW]
        for b, conv in filtered(matrix, product_ref, -128, convs, masks, lanes):
            at = slice(STEP * b, STEP * b + STEP)
            to = slice(STEP * (b - convs[0]), STEP * (b - convs[0]) + STEP)
            inner = conv + gain * product_ref[at, lanes].astype(F32)
            grad = (cot_ref[at, lanes].astype(F32) * inner).astype(BF16)
            gmix[0, to, :] = grad.astype(F32)
            gated_ref[to, lanes] = (mixed_ref[0, at, lanes].astype(F32) * inner).astype(BF16)
            if b == convs[0] or b == convs[-1]:
                half = STEP * (b == convs[-1])
                gmix_ref[0, half : half + STEP, lanes] = grad
        matrix = behind_ref[block, 0:WINDOW]
        for b, back in filtered(matrix, inner_ref, 0, backs, masks, lanes):
            at = slice(STEP * b, STEP * b + STEP)
            to = slice(STEP * (b - backs[0]), STEP * (b - backs[0]) + STEP)
            grad = back + gain * inner_ref[at, lanes].astype(F32)
            grad = grad.astype(BF16).astype(F32)
            for i, other in ((1, 2), (2, 1)):
                value = (grad * mixed_ref[other, at, lanes].astype(F32)).astype(BF16)
                gmix[i, to, :] = value.astype(F32)
                if b == backs[0] or b == backs[-1]:
                    half = STEP * (b == backs[-1])
                    gmix_ref[i, half : half + STEP, lanes] = value
        for i in range(3):
            totals = [None] * 7
            for lo in (0, 48):
                at = starts[i] + lo
                own = feat_ref[i, at : at + 48, lanes].astype(F32)
                grad_ref[i, lo : lo + 48, lanes] = short_pass(
                    gmix, i, own, weights, totals, lo, 48
                )
            lines = [jnp.sum(total, axis=0, keepdims=True) for total in totals]
            lines.append(jnp.zeros((1, LANES), F32))
            lines_ref[8 * i : 8 * i + 8, lanes] = jnp.concatenate(lines, axis=0)
        grid_ref[block, 0:WINDOW] = correlated(
            None,
            lambda b: product_ref[STEP * b : STEP * b + STEP, lanes],
            lambda b: inner_ref[STEP * b : STEP * b + WINDOW, lanes],
            backs,
            keep,
        )


def main_kernel(
    feat_ref, cot_ref, taps_ref, gain_ref, mixed_ref, product_ref, inner_ref, ahead_ref, behind_ref,
    near_gated, near_grad, near_gmix, lines_ref, grid_ref, up_ref, down_ref,
    gated_ref, grad_ref, sums_ref,
    prod, ginn, gmix, raw, edges, corr,
):
    step = pl.program_id(0)
    rows = cot_ref.shape[0]
    chunks = rows // STEP
    lanes = lanes_of(step)
    block = pl.ds(pl.multiple_of(LANES * step, LANES), LANES)
    every = pl.ds(0, LANES)
    weights = taps_ref[:, lanes]
    gain = gain_ref[:, lanes].astype(F32)
    masks = group_masks()
    keep = [m.astype(F32).astype(BF16) for m in masks]

    before = up_ref[128:160, lanes].astype(F32)
    tail = down_ref[128:160, lanes].astype(F32)
    start, end = [], []
    for i in range(3):
        raw[i, 0:8, :] = before[8 * i : 8 * i + 8]
        raw[i, 8:24, :] = feat_ref[i, 0:16, lanes].astype(F32)
        raw[i, 24:40, :] = feat_ref[i, rows - 16 : rows, lanes].astype(F32)
        raw[i, 40:48, :] = tail[8 + 8 * i : 16 + 8 * i]
        first = causal(raw, i, 8, 8, weights).astype(F32)
        second = mixed_ref[i, 0:16, lanes].astype(F32)[8:16]
        start.append(jnp.concatenate([first, second], axis=0))
        past_end = causal(raw, i, 40, 8, weights).astype(F32)
        end.append(jnp.concatenate([past_end, jnp.zeros((8, LANES), F32)], axis=0))
        edges[i, 0:16, :] = start[i]
        edges[i, 16:32, :] = end[i]
    opening = down_ref[0:16, lanes].astype(F32)
    past = iota((STEP, LANES), 0) < 6
    after = jnp.where(past, opening, 0.0)
    edges[3, 0:16, :] = cot_ref[0:16, lanes].astype(F32)
    edges[3, 16:32, :] = after

    prod[0:128, :] = up_ref[0:128, lanes]
    prod[128:144, :] = (start[1] * start[2]).astype(BF16)
    prod[144 : 128 + rows, :] = product_ref[16:rows, lanes]
    prod[128 + rows : 144 + rows, :] = (end[1] * end[2]).astype(BF16)
    ginn[0:16, :] = (cot_ref[0:16, lanes].astype(F32) * start[0]).astype(BF16)
    ginn[16:rows, :] = inner_ref[16:rows, lanes]
    ginn[rows : rows + 16, :] = jnp.where(past, after * end[0], opening).astype(BF16)
    ginn[rows + 16 : rows + 128, :] = down_ref[16:128, lanes]
    ginn[rows + 128 : rows + 144, :] = jnp.concatenate(
        [tail[0:8], jnp.zeros((8, LANES), F32)], axis=0
    ).astype(BF16)

    convs, backs = inside(rows)
    grid = correlated(
        grid_ref[block, 0:WINDOW],
        lambda b: prod[128 + STEP * b : 144 + STEP * b, :],
        lambda b: ginn[STEP * b : STEP * b + WINDOW, :],
        [b for b in range(chunks) if b not in backs],
        keep,
    )
    corr[0] = grid[:, 0:128]
    corr[1, :, 0 : WINDOW - 128] = grid[:, 128:WINDOW]
    corr[1, :, WINDOW - 128 : 128] = jnp.zeros((LANES, 256 - WINDOW), F32)

    def mixed(i, b):
        if b == 0 or b == chunks:
            return edges[i, STEP * (b > 0) : STEP * (b > 0) + STEP, :]
        if i == 3:
            return cot_ref[STEP * b : STEP * b + STEP, lanes].astype(F32)
        return mixed_ref[i, STEP * b : STEP * b + STEP, lanes].astype(F32)

    def put(i, b, values):
        gmix[i, STEP * b : STEP * b + STEP, :] = values.astype(BF16).astype(F32)

    outer = [b for b in range(chunks + 1) if b not in convs]
    for b, conv in filtered(ahead_ref[block, 0:WINDOW], prod, 0, outer, masks, every):
        inner = conv + gain * prod[128 + STEP * b : 144 + STEP * b, :].astype(F32)
        put(0, b, mixed(3, b) * inner)
        if b < chunks:
            gated_ref[STEP * b : STEP * b + STEP, :] = (mixed(0, b) * inner).astype(BF16)
    gated_ref[STEP * convs[0] : STEP * chunks, :] = near_gated[:, lanes]
    outer = [b for b in range(chunks + 1) if b not in backs]
    for b, back in filtered(behind_ref[block, 0:WINDOW], ginn, 0, outer, masks, every):
        grad = back + gain * ginn[STEP * b : STEP * b + STEP, :].astype(F32)
        grad = grad.astype(BF16).astype(F32)
        put(1, b, grad * mixed(2, b))
        put(2, b, grad * mixed(1, b))
    for i, known in ((0, convs), (1, backs), (2, backs)):
        put(i, known[0], near_gmix[i, 0:16, lanes])
        put(i, known[-1], near_gmix[i, 16:32, lanes])

    skip = jnp.zeros((STEP, LANES), F32)
    for b in range(chunks):
        p = prod[128 + STEP * b : 144 + STEP * b, :].astype(F32)
        skip = skip + p * ginn[STEP * b : STEP * b + STEP, :].astype(F32)
    sums_ref[pl.ds(64 + step, 1), :] = jnp.sum(skip, axis=0, keepdims=True)
    total = None
    for r in range(STEP):
        line = jnp.concatenate(
            [corr[half, pl.ds(r, GROUPS, stride=STEP), :] for half in (0, 1)], axis=1
        )
        line = line if r == 0 else pltpu.roll(line, 256 - r, 1)
        total = line[:, 0:128] if total is None else total + line[:, 0:128]
    sums_ref[pl.ds(pl.multiple_of(GROUPS * step, GROUPS), GROUPS), :] = total

    lines = []
    for i, first in enumerate(settled(rows)):
        totals = [None] * 7
        todo = [(0, first), (first + 96, rows)]
        for low, high in todo:
            for lo in range(low, high, 48):
                size = min(48, high - lo)
                own = feat_ref[i, lo : lo + size, lanes].astype(F32)
                grad_ref[i, lo : lo + size, :] = short_pass(
                    gmix, i, own, weights, totals, lo, size
                )
        grad_ref[i, first : first + 96, :] = near_grad[i, :, lanes]
        lines += [jnp.sum(part, axis=0, keepdims=True) for part in totals]
        lines.append(jnp.zeros((1, LANES), F32))
    lines = jnp.concatenate(lines, axis=0) + lines_ref[:, lanes]
    gather = iota((LANES, LANES), 1) == GROUPS * step + iota((LANES, LANES), 0) // 16
    gather = gather.astype(F32)
    short = jnp.dot(lines, gather, precision=lax.Precision.HIGHEST, preferred_element_type=F32)

    @pl.when(step == 0)
    def _():
        sums_ref[72:96, :] = short

    @pl.when(step > 0)
    def _():
        sums_ref[72:96, :] += short


def final_kernel(group_scale, token_scale, sums_ref, short_ref, long_ref, skip_ref):
    groups = long_ref.shape[0]
    values = sums_ref[...]
    long_ref[...] = values[0:groups] * group_scale
    skip_ref[...] = values[64 : 64 + skip_ref.shape[0]] * token_scale
    for i in range(3):
        short_ref[i] = values[72 + 8 * i : 79 + 8 * i, 0:groups] * group_scale


def blocks3(rows):
    return pl.BlockSpec((3, rows, LANES), lambda b: (0, 0, b))


def blocks2(rows):
    return pl.BlockSpec((rows, LANES), lambda b: (0, b))


def swap(values, axes):
    return lax.all_to_all(values, axes, 0, 0, tiled=True)


def summed(local):
    near, far = CTX[:2], CTX[2]
    parts = lax.axis_size(near)
    size = lax.axis_size(far)
    share = local.reshape(parts, -1, LANES)
    share = swap(share, near).sum(axis=0)
    every = jnp.broadcast_to(share[None], (size,) + share.shape)
    share = swap(every, far).sum(axis=0)
    every = jnp.broadcast_to(share[None], (parts,) + share.shape)
    return swap(every, near).reshape(local.shape)


def body(features, short_taps, long_taps, skip_gain, cotangent):
    rows, width = features.shape[1:]
    groups = width // 16
    steps = width // LANES
    inside_vmem = pl.BlockSpec(memory_space=pltpu.VMEM)
    outside = pl.BlockSpec(memory_space=pltpu.HBM)
    short_taps = short_taps.transpose(0, 2, 1)
    shape = jax.ShapeDtypeStruct

    def call(kernel, name, ins, outs, scratch, cost, grid=(), limit=LIMIT):
        return pl.pallas_call(
            kernel,
            grid=grid,
            in_specs=ins,
            out_specs=[spec for spec, _ in outs],
            out_shape=[out for _, out in outs],
            scratch_shapes=scratch,
            compiler_params=pltpu.CompilerParams(
                dimension_semantics=("arbitrary",) * len(grid), vmem_limit_bytes=limit
            ),
            cost_estimate=pl.CostEstimate(flops=cost, bytes_accessed=cost, transcendentals=0),
            name=name,
        )

    def held(*dims, dtype=BF16):
        return inside_vmem, shape(dims, dtype)

    up, down, taps = call(
        edge_kernel,
        "edge",
        [outside] * 3,
        [
            held(160, width),
            held(160, width),
            held(24, width, dtype=F32),
        ],
        [
            pltpu.VMEM((3, 144, width), BF16),
            pltpu.VMEM((3, 144, width), BF16),
            pltpu.VMEM((144, width), BF16),
            pltpu.VMEM(short_taps.shape, BF16),
            pltpu.VMEM((3, 152, LANES), F32),
            pltpu.SemaphoreType.DMA((8,)),
        ],
        5 * 10**6,
        limit=EDGE_LIMIT,
    )(features, cotangent, short_taps)
    from_last = passed_along(up, CTX, 1)
    from_next = passed_along(down, CTX, -1)
    convs, backs = inside(rows)
    gain = skip_gain.reshape(1, width)
    near = call(
        local_kernel,
        "local",
        [inside_vmem] * 5,
        [
            held(3, rows, width),
            held(rows, width),
            held(rows, width),
            held(groups * 16, 256),
            held(groups * 16, 256),
            held(STEP * len(convs), width),
            held(3, 96, width),
            held(3, 32, width),
            held(24, width, dtype=F32),
            held(groups * 16, 256, dtype=F32),
        ],
        [
            pltpu.VMEM((3, rows + 8, LANES), F32),
            pltpu.VMEM((2, groups, 256), F32),
            pltpu.VMEM((2, 2, 128, LANES), F32),
            pltpu.VMEM((3, STEP * len(convs), LANES), F32),
        ],
        2 * 10**7,
    )(features, cotangent, taps, long_taps, gain)
    gated, feature_grad, sums = call(
        main_kernel,
        "main",
        [inside_vmem] * 16,
        [
            (blocks2(rows), shape((rows, width), BF16)),
            (blocks3(rows), shape((3, rows, width), BF16)),
            (inside_vmem, shape((96, LANES), F32)),
        ],
        [
            pltpu.VMEM((rows + 144, LANES), BF16),
            pltpu.VMEM((rows + 144, LANES), BF16),
            pltpu.VMEM((3, rows + 16, LANES), F32),
            pltpu.VMEM((3, 48, LANES), F32),
            pltpu.VMEM((4, 32, LANES), F32),
            pltpu.VMEM((2, 128, LANES), F32),
        ],
        2 * 10**7,
        (steps,),
    )(features, cotangent, taps, gain, *near, from_last, from_next)
    tokens = rows * lax.axis_size(CTX)
    group_scale = 1.0 / math.sqrt(16.0 * tokens)
    token_scale = 1.0 / math.sqrt(1.0 * tokens)
    short, long, skip = call(
        functools.partial(final_kernel, group_scale, token_scale),
        "final",
        [inside_vmem],
        [
            held(3, 7, groups, dtype=F32),
            held(groups, LANES, dtype=F32),
            held(steps, LANES, dtype=F32),
        ],
        [],
        10**5,
    )(summed(sums))
    return gated, feature_grad, short.transpose(0, 2, 1), long, skip.reshape(width)


def solution(mesh):
    torus = Mesh(mesh.devices.reshape(*SPLIT, mesh.shape["tp"]), CTX + ("tp",))
    return jax.shard_map(
        body,
        mesh=torus,
        in_specs=(P(None, CTX, "tp"), P(None, "tp", None), P("tp", None), P("tp"), P(CTX, "tp")),
        out_specs=(P(CTX, "tp"), P(None, CTX, "tp"), P(None, "tp", None), P("tp", None), P("tp")),
        check_vma=False,
    )
```

```python
import functools
import math

import jax
import jax.numpy as jnp
from jax import lax
from jax.experimental import pallas as pl
from jax.experimental.pallas import tpu as pltpu
from jax.sharding import Mesh
from jax.sharding import PartitionSpec as P

CTX = ("ctx_0", "ctx_1", "ctx_2")
SPLIT = (4, 3, 8)
LANES = 128
GROUPS = 8
STEP = 16
WINDOW = 144
BF16 = jnp.bfloat16
F32 = jnp.float32
LIMIT = 16 * 2**20
TOGETHER, AT_EDGE, AT_LOCAL = 2, 4, 1
EDGE_LIMIT = 60000 * 2**10


def passed_along(block, axis, distance):
    devices = range(lax.axis_size(axis))
    route = [(i - distance, i) for i in devices if i - distance in devices]
    return lax.ppermute(block, axis, route)


def iota(shape, dim):
    return lax.broadcasted_iota(jnp.int32, shape, dim)


def lanes_of(step):
    return pl.ds(pl.multiple_of(LANES * step, LANES), LANES)


def channel_taps(taps_ref, out_ref):
    shape = (taps_ref.shape[2], out_ref.shape[1])
    spread = iota(shape, 0) == iota(shape, 1) // 16
    spread = spread.astype(F32).astype(BF16)
    for i in range(3):
        out_ref[8 * i : 8 * i + 7, :] = jnp.dot(
            taps_ref[i], spread, preferred_element_type=F32
        )


def part(refs, u):
    return [ref.at[u] for ref in refs]


def causal(ref, i, start, rows, taps):
    total = None
    for j in range(7):
        term = taps[8 * i + j : 8 * i + j + 1, :] * ref[i, start - j : start - j + rows, :]
        total = term if total is None else total + term
    return total.astype(BF16)


def pick_groups(full, masks):
    total = full[0:STEP]
    for g in range(1, GROUPS):
        total = jnp.where(masks[g], full[STEP * g : STEP * g + STEP], total)
    return total


def group_masks():
    group_of = iota((STEP, LANES), 1) // 16
    return [group_of == g for g in range(GROUPS)]


def filtered(matrix, ref, shift, chunks, masks, lanes):
    for at in range(0, len(chunks), 2):
        own = chunks[at : at + 2]
        parts = [ref[STEP * b + shift : STEP * b + shift + WINDOW, lanes] for b in own]
        parts = parts[0] if len(parts) == 1 else jnp.concatenate(parts, axis=1)
        full = jnp.dot(matrix, parts, preferred_element_type=F32)
        for n, b in enumerate(own):
            yield b, pick_groups(full[:, LANES * n : LANES * n + LANES], masks)


def inside(rows):
    chunks = rows // STEP
    return list(range(9, chunks)), list(range(1, chunks - 8))


def correlated(grid, products, inners, chunks, keep):
    for at in range(0, len(chunks), 2):
        own = chunks[at : at + 2]
        pieces = [products(b) for b in own]
        windows = [inners(b) for b in own]
        right = windows[0] if len(own) == 1 else jnp.concatenate(windows, axis=1)
        left = []
        for k in keep:
            masked = [k * p for p in pieces]
            left.append(masked[0] if len(own) == 1 else jnp.concatenate(masked, axis=1))
        term = lax.dot_general(
            jnp.concatenate(left, axis=0), right, (((1,), (1,)), ((), ())),
            preferred_element_type=F32,
        )
        grid = term if grid is None else grid + term
    return grid


def short_pass(gmix, i, own, weights, totals, lo, size):
    grad = None
    for j in range(7):
        moved = gmix[i, lo + j : lo + j + size, :]
        term = weights[8 * i + j : 8 * i + j + 1, :] * moved
        grad = term if grad is None else grad + term
        both = (moved * own).reshape(size // 8, 8, LANES).sum(axis=0)
        totals[j] = both if totals[j] is None else totals[j] + both
    return grad.astype(BF16)


def settled(rows):
    return [rows - 112, 16, 16]


def edge_kernel(
    feat_hbm, cot_hbm, taps_hbm, up_ref, down_ref, taps, opens, closes, cot_ref, taps_ref, raws, sems,
):
    rows = cot_hbm.shape[0]

    def block(step, raw):
        lanes = lanes_of(step)
        weights = taps[:, lanes]
        raw[0, 0:8, :] = jnp.zeros((8, LANES), F32)
        raw[0, 8:152, :] = opens[0, :, lanes].astype(F32)
        for i in (1, 2):
            raw[i, 0:144, :] = closes[i, :, lanes].astype(F32)
        for lo in (0, 64):
            key = causal(raw, 1, 16 + lo, 64, weights).astype(F32)
            value = causal(raw, 2, 16 + lo, 64, weights).astype(F32)
            up_ref[lo : lo + 64, lanes] = (key * value).astype(BF16)
        last = [closes[i, 128:144, lanes].astype(F32)[8:16] for i in range(3)]
        blank = jnp.zeros((8, LANES), F32)
        up_ref[128:160, lanes] = jnp.concatenate(last + [blank], axis=0).astype(BF16)
        for lo in (0, 64):
            inner = causal(raw, 0, 8 + lo, 64, weights).astype(F32)
            grad = cot_ref[lo : lo + 64, lanes].astype(F32)
            inner = grad * inner
            if lo == 0:
                first = jnp.where(iota((8, LANES), 0) < 6, grad[0:8], inner[0:8])
                inner = jnp.concatenate([first, inner[8:64]], axis=0)
            down_ref[lo : lo + 64, lanes] = inner.astype(BF16)
        query = causal(raw, 0, 136, 8, weights).astype(F32)
        rest = cot_ref[128:144, lanes].astype(F32)[0:8] * query
        begin = [opens[i, 0:16, lanes].astype(F32)[0:8] for i in range(3)]
        down_ref[128:160, lanes] = jnp.concatenate([rest] + begin, axis=0).astype(BF16)

    pairs = [
        (taps_hbm, taps_ref),
        (feat_hbm.at[1, rows - 144 : rows], closes.at[1]),
        (feat_hbm.at[2, rows - 144 : rows], closes.at[2]),
        (feat_hbm.at[0, 0:144], opens.at[0]),
        (cot_hbm.at[0:144], cot_ref),
        (feat_hbm.at[0, rows - 16 : rows], closes.at[0, 128:144]),
        (feat_hbm.at[1, 0:16], opens.at[1, 0:16]),
        (feat_hbm.at[2, 0:16], opens.at[2, 0:16]),
    ]
    copies = [
        pltpu.make_async_copy(source, target, sems.at[n])
        for n, (source, target) in enumerate(pairs)
    ]
    for copy in copies:
        copy.start()
    copies[0].wait()
    channel_taps(taps_ref, taps)
    for copy in copies[1:]:
        copy.wait()

    @pl.loop(0, cot_ref.shape[1] // LANES // AT_EDGE)
    def _(step):
        for u in range(AT_EDGE):
            block(AT_EDGE * step + u, raws.at[u])


def local_kernel(
    feat_ref, cot_ref, taps_ref, long_ref, gain_ref,
    taps_out, mixed_ref, product_ref, inner_ref, ahead_ref, behind_ref,
    gated_ref, grad_ref, gmix_ref, lines_ref, grid_ref,
    raws, filt, spreads, gmixes,
):
    rows = cot_ref.shape[0]
    groups = long_ref.shape[0]
    flip = iota((128, 256), 0) + iota((128, 256), 1) == 128
    flip = flip.astype(F32).astype(BF16)
    filt[0] = jnp.dot(long_ref[...], flip, preferred_element_type=F32)
    filt[1, :, 0:128] = long_ref[...].astype(F32)
    filt[1, :, 128:256] = jnp.zeros((groups, 128), F32)

    channel_taps(taps_ref, taps_out)

    def one(step, raw, spread, gmix):
        lanes = lanes_of(step)
        block = pl.ds(pl.multiple_of(LANES * step, LANES), LANES)
        gain = gain_ref[:, lanes].astype(F32)
        weights = taps_out[:, lanes]
        for which, out in ((0, ahead_ref), (1, behind_ref)):
            base = filt[which, pl.ds(pl.multiple_of(GROUPS * step, GROUPS), GROUPS), :]
            for r in range(STEP):
                moved = base if r == 0 else pltpu.roll(base, r, 1)
                for half in (0, 1):
                    part = moved[:, 128 * half : 128 * half + 128]
                    spread[which, half, pl.ds(r, GROUPS, stride=STEP), :] = part
            for half in (0, 1):
                out[block, 128 * half : 128 * half + 128] = spread[which, half].astype(BF16)
        for i in range(3):
            raw[i, 0:8, :] = jnp.zeros((8, LANES), F32)
            raw[i, 8 : 8 + rows, :] = feat_ref[i, :, lanes].astype(F32)
        size = 64
        for lo in range(0, rows, size):
            query, key, value = [causal(raw, i, 8 + lo, size, weights) for i in range(3)]
            mixed_ref[0, lo : lo + size, lanes] = query
            mixed_ref[1, lo : lo + size, lanes] = key
            mixed_ref[2, lo : lo + size, lanes] = value
            both = key.astype(F32) * value.astype(F32)
            product_ref[lo : lo + size, lanes] = both.astype(BF16)
            grad = cot_ref[lo : lo + size, lanes].astype(F32)
            inner_ref[lo : lo + size, lanes] = (grad * query.astype(F32)).astype(BF16)
        masks = group_masks()
        keep = [m.astype(F32).astype(BF16) for m in masks]
        convs, backs = inside(rows)
        starts = settled(rows)
        matrix = ahead_ref[block, 0:WINDOW]
        for b, conv in filtered(matrix, product_ref, -128, convs, masks, lanes):
            at = slice(STEP * b, STEP * b + STEP)
            to = slice(STEP * (b - convs[0]), STEP * (b - convs[0]) + STEP)
            inner = conv + gain * product_ref[at, lanes].astype(F32)
            grad = (cot_ref[at, lanes].astype(F32) * inner).astype(BF16)
            gmix[0, to, :] = grad.astype(F32)
            gated_ref[to, lanes] = (mixed_ref[0, at, lanes].astype(F32) * inner).astype(BF16)
            if b == convs[0] or b == convs[-1]:
                half = STEP * (b == convs[-1])
                gmix_ref[0, half : half + STEP, lanes] = grad
        matrix = behind_ref[block, 0:WINDOW]
        for b, back in filtered(matrix, inner_ref, 0, backs, masks, lanes):
            at = slice(STEP * b, STEP * b + STEP)
            to = slice(STEP * (b - backs[0]), STEP * (b - backs[0]) + STEP)
            grad = back + gain * inner_ref[at, lanes].astype(F32)
            grad = grad.astype(BF16).astype(F32)
            for i, other in ((1, 2), (2, 1)):
                value = (grad * mixed_ref[other, at, lanes].astype(F32)).astype(BF16)
                gmix[i, to, :] = value.astype(F32)
                if b == backs[0] or b == backs[-1]:
                    half = STEP * (b == backs[-1])
                    gmix_ref[i, half : half + STEP, lanes] = value
        for i in range(3):
            totals = [None] * 7
            for lo in (0, 48):
                at = starts[i] + lo
                own = feat_ref[i, at : at + 48, lanes].astype(F32)
                grad_ref[i, lo : lo + 48, lanes] = short_pass(
                    gmix, i, own, weights, totals, lo, 48
                )
            lines = [jnp.sum(total, axis=0, keepdims=True) for total in totals]
            lines.append(jnp.zeros((1, LANES), F32))
            lines_ref[8 * i : 8 * i + 8, lanes] = jnp.concatenate(lines, axis=0)
        grid_ref[block, 0:WINDOW] = correlated(
            None,
            lambda b: product_ref[STEP * b : STEP * b + STEP, lanes],
            lambda b: inner_ref[STEP * b : STEP * b + WINDOW, lanes],
            backs,
            keep,
        )

    @pl.loop(0, cot_ref.shape[1] // LANES // AT_LOCAL)
    def _(step):
        for u in range(AT_LOCAL):
            one(AT_LOCAL * step + u, *part((raws, spreads, gmixes), u))


def finish(gmix, i, low, high, shift, feat_ref, lanes, weights, totals, store):
    for lo in range(low, high, 48):
        size = min(48, high - lo)
        own = feat_ref[i, lo : lo + size, lanes].astype(F32)
        store(lo, size, short_pass(gmix, i, own, weights, totals, lo - shift, size))


def summed_lines(totals):
    lines = []
    for parts in totals:
        lines += [jnp.sum(part, axis=0, keepdims=True) for part in parts]
        lines.append(jnp.zeros((1, LANES), F32))
    return jnp.concatenate(lines, axis=0)


def before_block(
    step, feat_ref, cot_ref, taps_ref, gain_ref, mixed_ref, product_ref, inner_ref, ahead_ref, behind_ref,
    near_gated, near_gmix, lines_ref, grid_ref, up_ref,
    gated_ref, first_ref, grad_ref, lines_out, grid_out,
    prod, ginn, gmix, raw,
):
    rows = cot_ref.shape[0]
    lanes = lanes_of(step)
    block = pl.ds(pl.multiple_of(LANES * step, LANES), LANES)
    every = pl.ds(0, LANES)
    weights = taps_ref[:, lanes]
    gain = gain_ref[:, lanes].astype(F32)
    masks = group_masks()
    keep = [m.astype(F32).astype(BF16) for m in masks]
    convs, backs = inside(rows)

    before = up_ref[128:160, lanes].astype(F32)
    start = []
    for i in range(3):
        raw[i, 0:8, :] = before[8 * i : 8 * i + 8]
        raw[i, 8:24, :] = feat_ref[i, 0:16, lanes].astype(F32)
        first = causal(raw, i, 8, 8, weights).astype(F32)
        second = mixed_ref[i, 0:16, lanes].astype(F32)[8:16]
        start.append(jnp.concatenate([first, second], axis=0))
    product = (start[1] * start[2]).astype(BF16)
    inners = (cot_ref[0:16, lanes].astype(F32) * start[0]).astype(BF16)
    first_ref[0, :, lanes] = product
    first_ref[1, :, lanes] = inners
    prod[0:128, :] = up_ref[0:128, lanes]
    prod[128:144, :] = product
    prod[144:272, :] = product_ref[16:144, lanes]
    ginn[0:16, :] = inners
    ginn[16:144, :] = inner_ref[16:144, lanes]

    grid_out[block, 0:WINDOW] = correlated(
        grid_ref[block, 0:WINDOW], lambda b: product, lambda b: ginn[...], [0], keep
    )
    outer = list(range(convs[0]))
    for b, conv in filtered(ahead_ref[block, 0:WINDOW], prod, 0, outer, masks, every):
        at = slice(STEP * b, STEP * b + STEP)
        inner = conv + gain * prod[128 + STEP * b : 144 + STEP * b, :].astype(F32)
        query = start[0] if b == 0 else mixed_ref[0, at, lanes].astype(F32)
        gmix[0, at, :] = (cot_ref[at, lanes].astype(F32) * inner).astype(BF16).astype(F32)
        gated_ref[at, :] = (query * inner).astype(BF16)
    gated_ref[STEP * convs[0] : rows, :] = near_gated[:, lanes]
    for b, back in filtered(behind_ref[block, 0:WINDOW], ginn, 0, [0], masks, every):
        grad = back + gain * inners.astype(F32)
        grad = grad.astype(BF16).astype(F32)
        gmix[1, 0:16, :] = (grad * start[2]).astype(BF16).astype(F32)
        gmix[2, 0:16, :] = (grad * start[1]).astype(BF16).astype(F32)
    totals = [[None] * 7 for _ in range(3)]
    for i, known in enumerate(settled(rows)):
        gmix[i, known : known + 16, :] = near_gmix[i, 0:16, lanes].astype(F32)

        def store(lo, size, grad):
            grad_ref[i, lo : lo + size, lanes] = grad

        finish(gmix, i, 0, known, 0, feat_ref, lanes, weights, totals[i], store)
    lines_out[:, lanes] = lines_ref[:, lanes] + summed_lines(totals)


def after_block(
    step, feat_ref, taps_ref, gain_ref, mixed_ref, product_ref, inner_ref, ahead_ref, behind_ref,
    near_grad, near_gmix, first_ref, early_grad, lines_ref, grid_ref, down_ref,
    grad_ref, sums_ref,
    prod, ginn, gmix, raw, corr,
):
    rows = feat_ref.shape[1]
    chunks = rows // STEP
    lanes = lanes_of(step)
    block = pl.ds(pl.multiple_of(LANES * step, LANES), LANES)
    every = pl.ds(0, LANES)
    weights = taps_ref[:, lanes]
    gain = gain_ref[:, lanes].astype(F32)
    masks = group_masks()
    keep = [m.astype(F32).astype(BF16) for m in masks]
    convs, backs = inside(rows)
    base = rows - 128

    tail = down_ref[128:160, lanes].astype(F32)
    end = []
    for i in range(3):
        raw[i, 0:16, :] = feat_ref[i, rows - 16 : rows, lanes].astype(F32)
        raw[i, 16:24, :] = tail[8 + 8 * i : 16 + 8 * i]
        past_end = causal(raw, i, 16, 8, weights).astype(F32)
        end.append(jnp.concatenate([past_end, jnp.zeros((8, LANES), F32)], axis=0))
    opening = down_ref[0:16, lanes].astype(F32)
    past = iota((STEP, LANES), 0) < 6
    after = jnp.where(past, opening, 0.0)
    prod[0:128, :] = product_ref[base:rows, lanes]
    prod[128:144, :] = (end[1] * end[2]).astype(BF16)
    ginn[0:128, :] = inner_ref[base:rows, lanes]
    ginn[128:144, :] = jnp.where(past, after * end[0], opening).astype(BF16)
    ginn[144:256, :] = down_ref[16:128, lanes]
    ginn[256:272, :] = jnp.concatenate(
        [tail[0:8], jnp.zeros((8, LANES), F32)], axis=0
    ).astype(BF16)

    outer = list(range(backs[-1] + 1, chunks))
    grid = correlated(
        grid_ref[block, 0:WINDOW],
        lambda b: prod[STEP * b - base : STEP * b - base + STEP, :],
        lambda b: ginn[STEP * b - base : STEP * b - base + WINDOW, :],
        outer,
        keep,
    )
    corr[0] = grid[:, 0:128]
    corr[1, :, 0 : WINDOW - 128] = grid[:, 128:WINDOW]
    corr[1, :, WINDOW - 128 : 128] = jnp.zeros((LANES, 256 - WINDOW), F32)

    shift = base - STEP
    for b, conv in filtered(ahead_ref[block, 0:WINDOW], prod, -base - 128, [chunks], masks, every):
        inner = conv + gain * prod[128:144, :].astype(F32)
        gmix[0, rows - shift : rows - shift + STEP, :] = (after * inner).astype(BF16).astype(F32)
    outer.append(chunks)
    for b, back in filtered(behind_ref[block, 0:WINDOW], ginn, -base, outer, masks, every):
        at = slice(STEP * b, STEP * b + STEP)
        to = slice(STEP * b - shift, STEP * b - shift + STEP)
        grad = back + gain * ginn[STEP * b - base : STEP * b - base + STEP, :].astype(F32)
        grad = grad.astype(BF16).astype(F32)
        for i, other in ((1, 2), (2, 1)):
            value = end[other] if b == chunks else mixed_ref[other, at, lanes].astype(F32)
            gmix[i, to, :] = (grad * value).astype(BF16).astype(F32)

    skip = first_ref[0, :, lanes].astype(F32) * first_ref[1, :, lanes].astype(F32)
    for lo in range(STEP, rows, STEP):
        p = product_ref[lo : lo + STEP, lanes].astype(F32)
        skip = skip + p * inner_ref[lo : lo + STEP, lanes].astype(F32)
    sums_ref[pl.ds(64 + step, 1), :] = jnp.sum(skip, axis=0, keepdims=True)
    total = None
    for r in range(STEP):
        line = jnp.concatenate(
            [corr[half, pl.ds(r, GROUPS, stride=STEP), :] for half in (0, 1)], axis=1
        )
        line = line if r == 0 else pltpu.roll(line, 256 - r, 1)
        total = line[:, 0:128] if total is None else total + line[:, 0:128]
    sums_ref[pl.ds(pl.multiple_of(GROUPS * step, GROUPS), GROUPS), :] = total

    totals = [[None] * 7 for _ in range(3)]
    for i, known in enumerate(settled(rows)):
        stop = known + 96
        gmix[i, stop - shift : stop - shift + STEP, :] = near_gmix[i, 16:32, lanes].astype(F32)

        def store(lo, size, grad):
            grad_ref[i, lo : lo + size, :] = grad

        finish(gmix, i, stop, rows, shift, feat_ref, lanes, weights, totals[i], store)
        grad_ref[i, 0:known, :] = early_grad[i, 0:known, lanes]
        grad_ref[i, known:stop, :] = near_grad[i, :, lanes]
    lines = summed_lines(totals) + lines_ref[:, lanes]
    gather = iota((LANES, LANES), 1) == GROUPS * step + iota((LANES, LANES), 0) // 16
    gather = gather.astype(F32)
    return jnp.dot(lines, gather, precision=lax.Precision.HIGHEST, preferred_element_type=F32)


def before_kernel(*refs):
    ins, (gated_ref, *outs), scratch = refs[:14], refs[14:19], refs[19:]
    for u in range(TOGETHER):
        gated = gated_ref.at[:, LANES * u : LANES * u + LANES]
        step = TOGETHER * pl.program_id(0) + u
        before_block(step, *ins, gated, *outs, *part(scratch, u))


def after_kernel(*refs):
    ins, (grad_ref, sums_ref), scratch = refs[:15], refs[15:17], refs[17:]
    first = pl.program_id(0) == 0
    short = jnp.where(first, 0.0, sums_ref[72:96, :])
    for u in range(TOGETHER):
        grad = grad_ref.at[:, :, LANES * u : LANES * u + LANES]
        step = TOGETHER * pl.program_id(0) + u
        short = short + after_block(step, *ins, grad, sums_ref, *part(scratch, u))
    sums_ref[72:96, :] = short


def final_kernel(group_scale, token_scale, sums_ref, short_ref, long_ref, skip_ref):
    groups = long_ref.shape[0]
    values = sums_ref[...]
    long_ref[...] = values[0:groups] * group_scale
    skip_ref[...] = values[64 : 64 + skip_ref.shape[0]] * token_scale
    for i in range(3):
        short_ref[i] = values[72 + 8 * i : 79 + 8 * i, 0:groups] * group_scale


def blocks3(rows):
    return pl.BlockSpec((3, rows, TOGETHER * LANES), lambda b: (0, 0, b))


def blocks2(rows):
    return pl.BlockSpec((rows, TOGETHER * LANES), lambda b: (0, b))


def swap(values, axes):
    return lax.all_to_all(values, axes, 0, 0, tiled=True)


def summed(local):
    near, far = CTX[:2], CTX[2]
    parts = lax.axis_size(near)
    size = lax.axis_size(far)
    share = local.reshape(parts, -1, LANES)
    share = swap(share, near).sum(axis=0)
    every = jnp.broadcast_to(share[None], (size,) + share.shape)
    share = swap(every, far).sum(axis=0)
    every = jnp.broadcast_to(share[None], (parts,) + share.shape)
    return swap(every, near).reshape(local.shape)


def body(features, short_taps, long_taps, skip_gain, cotangent):
    rows, width = features.shape[1:]
    groups = width // 16
    steps = width // LANES
    inside_vmem = pl.BlockSpec(memory_space=pltpu.VMEM)
    outside = pl.BlockSpec(memory_space=pltpu.HBM)
    short_taps = short_taps.transpose(0, 2, 1)
    shape = jax.ShapeDtypeStruct

    def call(kernel, name, ins, outs, scratch, cost, grid=(), limit=LIMIT):
        return pl.pallas_call(
            kernel,
            grid=grid,
            in_specs=ins,
            out_specs=[spec for spec, _ in outs],
            out_shape=[out for _, out in outs],
            scratch_shapes=scratch,
            compiler_params=pltpu.CompilerParams(
                dimension_semantics=("arbitrary",) * len(grid), vmem_limit_bytes=limit
            ),
            cost_estimate=pl.CostEstimate(flops=cost, bytes_accessed=cost, transcendentals=0),
            name=name,
        )

    def held(*dims, dtype=BF16):
        return inside_vmem, shape(dims, dtype)

    up, down = call(
        edge_kernel,
        "edge",
        [outside] * 3,
        [
            held(160, width),
            held(160, width),
        ],
        [
            pltpu.VMEM((24, width), F32),
            pltpu.VMEM((3, 144, width), BF16),
            pltpu.VMEM((3, 144, width), BF16),
            pltpu.VMEM((144, width), BF16),
            pltpu.VMEM(short_taps.shape, BF16),
            pltpu.VMEM((AT_EDGE, 3, 152, LANES), F32),
            pltpu.SemaphoreType.DMA((8,)),
        ],
        5 * 10**6,
        limit=EDGE_LIMIT,
    )(features, cotangent, short_taps)
    from_last = passed_along(up, CTX, 1)
    from_next = passed_along(down, CTX, -1)
    convs, backs = inside(rows)
    gain = skip_gain.reshape(1, width)
    mixers = [
        held(24, width, dtype=F32),
        held(3, rows, width),
        held(rows, width),
        held(rows, width),
        held(groups * 16, 256),
        held(groups * 16, 256),
    ]
    sums_so_far = [held(24, width, dtype=F32), held(groups * 16, 256, dtype=F32)]
    taps, mixed, product, inner, ahead, behind, near_gated, near_grad, near_gmix, *parts = call(
        local_kernel,
        "local",
        [inside_vmem] * 5,
        mixers
        + [held(STEP * len(convs), width), held(3, 96, width), held(3, 32, width)]
        + sums_so_far,
        [
            pltpu.VMEM((AT_LOCAL, 3, rows + 8, LANES), F32),
            pltpu.VMEM((2, groups, 256), F32),
            pltpu.VMEM((AT_LOCAL, 2, 2, 128, LANES), F32),
            pltpu.VMEM((AT_LOCAL, 3, STEP * len(convs), LANES), F32),
        ],
        2 * 10**7,
    )(features, cotangent, short_taps, long_taps, gain)
    most = STEP * convs[0]
    gated, first, early_grad, *parts = call(
        before_kernel,
        "before",
        [inside_vmem] * 14,
        [
            (blocks2(rows), shape((rows, width), BF16)),
            held(2, STEP, width),
            held(3, most, width),
        ]
        + sums_so_far,
        [
            pltpu.VMEM((TOGETHER, 272, LANES), BF16),
            pltpu.VMEM((TOGETHER, WINDOW, LANES), BF16),
            pltpu.VMEM((TOGETHER, 3, most + STEP, LANES), F32),
            pltpu.VMEM((TOGETHER, 3, 24, LANES), F32),
        ],
        10**7,
        (steps // TOGETHER,),
    )(
        features, cotangent, taps, gain, mixed, product, inner, ahead, behind, near_gated, near_gmix,
        *parts, from_last,
    )
    feature_grad, sums = call(
        after_kernel,
        "after",
        [inside_vmem] * 15,
        [
            (blocks3(rows), shape((3, rows, width), BF16)),
            (inside_vmem, shape((96, LANES), F32)),
        ],
        [
            pltpu.VMEM((TOGETHER, WINDOW, LANES), BF16),
            pltpu.VMEM((TOGETHER, 272, LANES), BF16),
            pltpu.VMEM((TOGETHER, 3, 160, LANES), F32),
            pltpu.VMEM((TOGETHER, 3, 24, LANES), F32),
            pltpu.VMEM((TOGETHER, 2, 128, LANES), F32),
        ],
        10**7,
        (steps // TOGETHER,),
    )(
        features, taps, gain, mixed, product, inner, ahead, behind, near_grad, near_gmix, first,
        early_grad, *parts, from_next,
    )
    tokens = rows * lax.axis_size(CTX)
    group_scale = 1.0 / math.sqrt(16.0 * tokens)
    token_scale = 1.0 / math.sqrt(1.0 * tokens)
    short, long, skip = call(
        functools.partial(final_kernel, group_scale, token_scale),
        "final",
        [inside_vmem],
        [
            held(3, 7, groups, dtype=F32),
            held(groups, LANES, dtype=F32),
            held(steps, LANES, dtype=F32),
        ],
        [],
        10**5,
    )(summed(sums))
    return gated, feature_grad, short.transpose(0, 2, 1), long, skip.reshape(width)


def solution(mesh):
    torus = Mesh(mesh.devices.reshape(*SPLIT, mesh.shape["tp"]), CTX + ("tp",))
    return jax.shard_map(
        body,
        mesh=torus,
        in_specs=(P(None, CTX, "tp"), P(None, "tp", None), P("tp", None), P("tp"), P(CTX, "tp")),
        out_specs=(P(CTX, "tp"), P(None, CTX, "tp"), P(None, "tp", None), P("tp", None), P("tp")),
        check_vma=False,
    )
```

```python
import functools
import math

import jax
import jax.numpy as jnp
from jax import lax
from jax.experimental import pallas as pl
from jax.experimental.pallas import tpu as pltpu
from jax.sharding import Mesh
from jax.sharding import PartitionSpec as P

CTX = ("ctx_0", "ctx_1", "ctx_2")
SPLIT = (4, 3, 8)
LANES = 128
GROUPS = 8
STEP = 16
WINDOW = 144
BF16 = jnp.bfloat16
F32 = jnp.float32
LIMIT = 16 * 2**20
TOGETHER, AT_EDGE, AT_LOCAL = 2, 4, 1
EDGE_LIMIT = 60000 * 2**10


def passed_along(block, axis, distance):
    devices = range(lax.axis_size(axis))
    route = [(i - distance, i) for i in devices if i - distance in devices]
    return lax.ppermute(block, axis, route)


def iota(shape, dim):
    return lax.broadcasted_iota(jnp.int32, shape, dim)


def lanes_of(step):
    if isinstance(step, int):
        return pl.ds(LANES * step, LANES)
    return pl.ds(pl.multiple_of(LANES * step, LANES), LANES)


def channel_taps(taps_ref, out_ref):
    shape = (taps_ref.shape[2], out_ref.shape[1])
    spread = iota(shape, 0) == iota(shape, 1) // 16
    spread = spread.astype(F32).astype(BF16)
    for i in range(3):
        out_ref[8 * i : 8 * i + 7, :] = jnp.dot(
            taps_ref[i], spread, preferred_element_type=F32
        )


def part(refs, u):
    return [ref.at[u] for ref in refs]


def causal(ref, i, start, rows, taps):
    total = None
    for j in range(7):
        term = taps[8 * i + j : 8 * i + j + 1, :] * ref[i, start - j : start - j + rows, :]
        total = term if total is None else total + term
    return total.astype(BF16)


def pick_groups(full, masks):
    total = full[0:STEP]
    for g in range(1, GROUPS):
        total = jnp.where(masks[g], full[STEP * g : STEP * g + STEP], total)
    return total


def group_masks():
    group_of = iota((STEP, LANES), 1) // 16
    return [group_of == g for g in range(GROUPS)]


def filtered(matrix, ref, shift, chunks, masks, lanes):
    for at in range(0, len(chunks), 2):
        own = chunks[at : at + 2]
        parts = [ref[STEP * b + shift : STEP * b + shift + WINDOW, lanes] for b in own]
        parts = parts[0] if len(parts) == 1 else jnp.concatenate(parts, axis=1)
        full = jnp.dot(matrix, parts, preferred_element_type=F32)
        for n, b in enumerate(own):
            yield b, pick_groups(full[:, LANES * n : LANES * n + LANES], masks)


def inside(rows):
    chunks = rows // STEP
    return list(range(9, chunks)), list(range(1, chunks - 8))


def correlated(grid, products, inners, chunks, keep):
    for at in range(0, len(chunks), 2):
        own = chunks[at : at + 2]
        pieces = [products(b) for b in own]
        windows = [inners(b) for b in own]
        right = windows[0] if len(own) == 1 else jnp.concatenate(windows, axis=1)
        left = []
        for k in keep:
            masked = [k * p for p in pieces]
            left.append(masked[0] if len(own) == 1 else jnp.concatenate(masked, axis=1))
        term = lax.dot_general(
            jnp.concatenate(left, axis=0), right, (((1,), (1,)), ((), ())),
            preferred_element_type=F32,
        )
        grid = term if grid is None else grid + term
    return grid


def short_pass(gmix, i, own, weights, totals, lo, size):
    grad = None
    for j in range(7):
        moved = gmix[i, lo + j : lo + j + size, :]
        term = weights[8 * i + j : 8 * i + j + 1, :] * moved
        grad = term if grad is None else grad + term
        both = (moved * own).reshape(size // 8, 8, LANES).sum(axis=0)
        totals[j] = both if totals[j] is None else totals[j] + both
    return grad.astype(BF16)


def settled(rows):
    return [rows - 112, 16, 16]


def edge_kernel(
    feat_hbm, cot_hbm, taps_hbm, up_hbm, down_hbm,
    up_ref, down_ref, taps, opens, closes, cot_ref, taps_ref, raws, sems, out_sems,
):
    rows, width = cot_hbm.shape
    span = AT_EDGE * LANES

    def block(step, raw):
        lanes = lanes_of(step)
        weights = taps[:, lanes]
        raw[0, 0:8, :] = jnp.zeros((8, LANES), F32)
        raw[0, 8:152, :] = opens[0, :, lanes].astype(F32)
        for i in (1, 2):
            raw[i, 0:144, :] = closes[i, :, lanes].astype(F32)
        for lo in (0, 64):
            key = causal(raw, 1, 16 + lo, 64, weights).astype(F32)
            value = causal(raw, 2, 16 + lo, 64, weights).astype(F32)
            up_ref[lo : lo + 64, lanes] = (key * value).astype(BF16)
        last = [closes[i, 128:144, lanes].astype(F32)[8:16] for i in range(3)]
        blank = jnp.zeros((8, LANES), F32)
        up_ref[128:160, lanes] = jnp.concatenate(last + [blank], axis=0).astype(BF16)
        for lo in (0, 64):
            inner = causal(raw, 0, 8 + lo, 64, weights).astype(F32)
            grad = cot_ref[lo : lo + 64, lanes].astype(F32)
            inner = grad * inner
            if lo == 0:
                first = jnp.where(iota((8, LANES), 0) < 6, grad[0:8], inner[0:8])
                inner = jnp.concatenate([first, inner[8:64]], axis=0)
            down_ref[lo : lo + 64, lanes] = inner.astype(BF16)
        query = causal(raw, 0, 136, 8, weights).astype(F32)
        rest = cot_ref[128:144, lanes].astype(F32)[0:8] * query
        begin = [opens[i, 0:16, lanes].astype(F32)[0:8] for i in range(3)]
        down_ref[128:160, lanes] = jnp.concatenate([rest] + begin, axis=0).astype(BF16)

    def fetches(at):
        lanes = pl.ds(span * at, span)
        pairs = [
            (feat_hbm.at[1, rows - 144 : rows, lanes], closes.at[1, :, lanes]),
            (feat_hbm.at[2, rows - 144 : rows, lanes], closes.at[2, :, lanes]),
            (feat_hbm.at[0, 0:144, lanes], opens.at[0, :, lanes]),
            (cot_hbm.at[0:144, lanes], cot_ref.at[:, lanes]),
            (feat_hbm.at[0, rows - 16 : rows, lanes], closes.at[0, 128:144, lanes]),
            (feat_hbm.at[1, 0:16, lanes], opens.at[1, 0:16, lanes]),
            (feat_hbm.at[2, 0:16, lanes], opens.at[2, 0:16, lanes]),
        ]
        return [
            pltpu.make_async_copy(source, target, sems.at[at, n])
            for n, (source, target) in enumerate(pairs)
        ]

    def stores(at):
        lanes = pl.ds(span * at, span)
        return [
            pltpu.make_async_copy(up_ref.at[:, lanes], up_hbm.at[:, lanes], out_sems.at[at, 0]),
            pltpu.make_async_copy(
                down_ref.at[:, lanes], down_hbm.at[:, lanes], out_sems.at[at, 1]
            ),
        ]

    turns = range(width // span)
    first = pltpu.make_async_copy(taps_hbm, taps_ref, sems.at[0, 7])
    first.start()
    for at in turns:
        for copy in fetches(at):
            copy.start()
    first.wait()
    channel_taps(taps_ref, taps)
    for at in turns:
        for copy in fetches(at):
            copy.wait()
        for u in range(AT_EDGE):
            block(AT_EDGE * at + u, raws.at[u])
        for copy in stores(at):
            copy.start()
    for at in turns:
        for copy in stores(at):
            copy.wait()


def local_kernel(
    feat_ref, cot_ref, taps_ref, long_ref, gain_ref,
    taps_out, gain_out, mixed_ref, product_ref, inner_ref, ahead_ref, behind_ref,
    gated_ref, grad_ref, gmix_ref, lines_ref, grid_ref,
    raws, filt, spreads, gmixes,
):
    rows = cot_ref.shape[0]
    groups = long_ref.shape[0]
    flip = iota((128, 256), 0) + iota((128, 256), 1) == 128
    flip = flip.astype(F32).astype(BF16)
    filt[0] = jnp.dot(long_ref[...], flip, preferred_element_type=F32)
    filt[1, :, 0:128] = long_ref[...].astype(F32)
    filt[1, :, 128:256] = jnp.zeros((groups, 128), F32)

    channel_taps(taps_ref, taps_out)
    gain_out[...] = gain_ref[...].astype(F32)

    def one(step, raw, spread, gmix):
        lanes = lanes_of(step)
        block = pl.ds(pl.multiple_of(LANES * step, LANES), LANES)
        gain = gain_out[pl.ds(step, 1), :]
        weights = taps_out[:, lanes]
        for which, out in ((0, ahead_ref), (1, behind_ref)):
            base = filt[which, pl.ds(pl.multiple_of(GROUPS * step, GROUPS), GROUPS), :]
            for r in range(STEP):
                moved = base if r == 0 else pltpu.roll(base, r, 1)
                for half in (0, 1):
                    part = moved[:, 128 * half : 128 * half + 128]
                    spread[which, half, pl.ds(r, GROUPS, stride=STEP), :] = part
            for half in (0, 1):
                out[block, 128 * half : 128 * half + 128] = spread[which, half].astype(BF16)
        for i in range(3):
            raw[i, 0:8, :] = jnp.zeros((8, LANES), F32)
            raw[i, 8 : 8 + rows, :] = feat_ref[i, :, lanes].astype(F32)
        size = 64
        for lo in range(0, rows, size):
            query, key, value = [causal(raw, i, 8 + lo, size, weights) for i in range(3)]
            mixed_ref[0, lo : lo + size, lanes] = query
            mixed_ref[1, lo : lo + size, lanes] = key
            mixed_ref[2, lo : lo + size, lanes] = value
            both = key.astype(F32) * value.astype(F32)
            product_ref[lo : lo + size, lanes] = both.astype(BF16)
            grad = cot_ref[lo : lo + size, lanes].astype(F32)
            inner_ref[lo : lo + size, lanes] = (grad * query.astype(F32)).astype(BF16)
        masks = group_masks()
        keep = [m.astype(F32).astype(BF16) for m in masks]
        convs, backs = inside(rows)
        starts = settled(rows)
        matrix = ahead_ref[block, 0:WINDOW]
        for b, conv in filtered(matrix, product_ref, -128, convs, masks, lanes):
            at = slice(STEP * b, STEP * b + STEP)
            to = slice(STEP * (b - convs[0]), STEP * (b - convs[0]) + STEP)
            inner = conv + gain * product_ref[at, lanes].astype(F32)
            grad = (cot_ref[at, lanes].astype(F32) * inner).astype(BF16)
            gmix[0, to, :] = grad.astype(F32)
            gated_ref[to, lanes] = (mixed_ref[0, at, lanes].astype(F32) * inner).astype(BF16)
            if b == convs[0] or b == convs[-1]:
                half = STEP * (b == convs[-1])
                gmix_ref[0, half : half + STEP, lanes] = grad
        matrix = behind_ref[block, 0:WINDOW]
        for b, back in filtered(matrix, inner_ref, 0, backs, masks, lanes):
            at = slice(STEP * b, STEP * b + STEP)
            to = slice(STEP * (b - backs[0]), STEP * (b - backs[0]) + STEP)
            grad = back + gain * inner_ref[at, lanes].astype(F32)
            grad = grad.astype(BF16).astype(F32)
            for i, other in ((1, 2), (2, 1)):
                value = (grad * mixed_ref[other, at, lanes].astype(F32)).astype(BF16)
                gmix[i, to, :] = value.astype(F32)
                if b == backs[0] or b == backs[-1]:
                    half = STEP * (b == backs[-1])
                    gmix_ref[i, half : half + STEP, lanes] = value
        for i in range(3):
            totals = [None] * 7
            for lo in (0, 48):
                at = starts[i] + lo
                own = feat_ref[i, at : at + 48, lanes].astype(F32)
                grad_ref[i, lo : lo + 48, lanes] = short_pass(
                    gmix, i, own, weights, totals, lo, 48
                )
            lines = [jnp.sum(total, axis=0, keepdims=True) for total in totals]
            lines.append(jnp.zeros((1, LANES), F32))
            lines_ref[8 * i : 8 * i + 8, lanes] = jnp.concatenate(lines, axis=0)
        grid_ref[block, 0:WINDOW] = correlated(
            None,
            lambda b: product_ref[STEP * b : STEP * b + STEP, lanes],
            lambda b: inner_ref[STEP * b : STEP * b + WINDOW, lanes],
            backs,
            keep,
        )

    @pl.loop(0, cot_ref.shape[1] // LANES // AT_LOCAL)
    def _(step):
        for u in range(AT_LOCAL):
            one(AT_LOCAL * step + u, *part((raws, spreads, gmixes), u))


def finish(gmix, i, low, high, shift, feat_ref, lanes, weights, totals, store):
    for lo in range(low, high, 48):
        size = min(48, high - lo)
        own = feat_ref[i, lo : lo + size, lanes].astype(F32)
        store(lo, size, short_pass(gmix, i, own, weights, totals, lo - shift, size))


def summed_lines(totals):
    lines = []
    for parts in totals:
        lines += [jnp.sum(part, axis=0, keepdims=True) for part in parts]
        lines.append(jnp.zeros((1, LANES), F32))
    return jnp.concatenate(lines, axis=0)


def before_block(
    step, feat_ref, cot_ref, taps_ref, gain_ref, mixed_ref, product_ref, inner_ref, ahead_ref, behind_ref,
    near_gated, near_gmix, lines_ref, grid_ref, up_ref,
    gated_ref, first_ref, grad_ref, lines_out, grid_out,
    prod, ginn, gmix, raw,
):
    rows = cot_ref.shape[0]
    lanes = lanes_of(step)
    block = pl.ds(pl.multiple_of(LANES * step, LANES), LANES)
    every = pl.ds(0, LANES)
    weights = taps_ref[:, lanes]
    gain = gain_ref[pl.ds(step, 1), :]
    masks = group_masks()
    keep = [m.astype(F32).astype(BF16) for m in masks]
    convs, backs = inside(rows)

    before = up_ref[128:160, lanes].astype(F32)
    start = []
    for i in range(3):
        raw[i, 0:8, :] = before[8 * i : 8 * i + 8]
        raw[i, 8:24, :] = feat_ref[i, 0:16, lanes].astype(F32)
        first = causal(raw, i, 8, 8, weights).astype(F32)
        second = mixed_ref[i, 0:16, lanes].astype(F32)[8:16]
        start.append(jnp.concatenate([first, second], axis=0))
    product = (start[1] * start[2]).astype(BF16)
    inners = (cot_ref[0:16, lanes].astype(F32) * start[0]).astype(BF16)
    first_ref[0, :, lanes] = product
    first_ref[1, :, lanes] = inners
    prod[0:128, :] = up_ref[0:128, lanes]
    prod[128:144, :] = product
    prod[144:272, :] = product_ref[16:144, lanes]
    ginn[0:16, :] = inners
    ginn[16:144, :] = inner_ref[16:144, lanes]

    grid_out[block, 0:WINDOW] = correlated(
        grid_ref[block, 0:WINDOW], lambda b: product, lambda b: ginn[...], [0], keep
    )
    outer = list(range(convs[0]))
    for b, conv in filtered(ahead_ref[block, 0:WINDOW], prod, 0, outer, masks, every):
        at = slice(STEP * b, STEP * b + STEP)
        inner = conv + gain * prod[128 + STEP * b : 144 + STEP * b, :].astype(F32)
        query = start[0] if b == 0 else mixed_ref[0, at, lanes].astype(F32)
        gmix[0, at, :] = (cot_ref[at, lanes].astype(F32) * inner).astype(BF16).astype(F32)
        gated_ref[at, :] = (query * inner).astype(BF16)
    gated_ref[STEP * convs[0] : rows, :] = near_gated[:, lanes]
    for b, back in filtered(behind_ref[block, 0:WINDOW], ginn, 0, [0], masks, every):
        grad = back + gain * inners.astype(F32)
        grad = grad.astype(BF16).astype(F32)
        gmix[1, 0:16, :] = (grad * start[2]).astype(BF16).astype(F32)
        gmix[2, 0:16, :] = (grad * start[1]).astype(BF16).astype(F32)
    totals = [[None] * 7 for _ in range(3)]
    for i, known in enumerate(settled(rows)):
        gmix[i, known : known + 16, :] = near_gmix[i, 0:16, lanes].astype(F32)

        def store(lo, size, grad):
            grad_ref[i, lo : lo + size, lanes] = grad

        finish(gmix, i, 0, known, 0, feat_ref, lanes, weights, totals[i], store)
    lines_out[:, lanes] = lines_ref[:, lanes] + summed_lines(totals)


def after_block(
    step, feat_ref, taps_ref, gain_ref, mixed_ref, product_ref, inner_ref, ahead_ref, behind_ref,
    near_grad, near_gmix, first_ref, early_grad, lines_ref, grid_ref, down_ref,
    grad_ref, sums_ref,
    prod, ginn, gmix, raw, corr,
):
    rows = feat_ref.shape[1]
    chunks = rows // STEP
    lanes = lanes_of(step)
    block = pl.ds(pl.multiple_of(LANES * step, LANES), LANES)
    every = pl.ds(0, LANES)
    weights = taps_ref[:, lanes]
    gain = gain_ref[pl.ds(step, 1), :]
    masks = group_masks()
    keep = [m.astype(F32).astype(BF16) for m in masks]
    convs, backs = inside(rows)
    base = rows - 128

    tail = down_ref[128:160, lanes].astype(F32)
    end = []
    for i in range(3):
        raw[i, 0:16, :] = feat_ref[i, rows - 16 : rows, lanes].astype(F32)
        raw[i, 16:24, :] = tail[8 + 8 * i : 16 + 8 * i]
        past_end = causal(raw, i, 16, 8, weights).astype(F32)
        end.append(jnp.concatenate([past_end, jnp.zeros((8, LANES), F32)], axis=0))
    opening = down_ref[0:16, lanes].astype(F32)
    past = iota((STEP, LANES), 0) < 6
    after = jnp.where(past, opening, 0.0)
    prod[0:128, :] = product_ref[base:rows, lanes]
    prod[128:144, :] = (end[1] * end[2]).astype(BF16)
    ginn[0:128, :] = inner_ref[base:rows, lanes]
    ginn[128:144, :] = jnp.where(past, after * end[0], opening).astype(BF16)
    ginn[144:256, :] = down_ref[16:128, lanes]
    ginn[256:272, :] = jnp.concatenate(
        [tail[0:8], jnp.zeros((8, LANES), F32)], axis=0
    ).astype(BF16)

    outer = list(range(backs[-1] + 1, chunks))
    grid = correlated(
        grid_ref[block, 0:WINDOW],
        lambda b: prod[STEP * b - base : STEP * b - base + STEP, :],
        lambda b: ginn[STEP * b - base : STEP * b - base + WINDOW, :],
        outer,
        keep,
    )
    corr[0] = grid[:, 0:128]
    corr[1, :, 0 : WINDOW - 128] = grid[:, 128:WINDOW]
    corr[1, :, WINDOW - 128 : 128] = jnp.zeros((LANES, 256 - WINDOW), F32)

    shift = base - STEP
    for b, conv in filtered(ahead_ref[block, 0:WINDOW], prod, -base - 128, [chunks], masks, every):
        inner = conv + gain * prod[128:144, :].astype(F32)
        gmix[0, rows - shift : rows - shift + STEP, :] = (after * inner).astype(BF16).astype(F32)
    outer.append(chunks)
    for b, back in filtered(behind_ref[block, 0:WINDOW], ginn, -base, outer, masks, every):
        at = slice(STEP * b, STEP * b + STEP)
        to = slice(STEP * b - shift, STEP * b - shift + STEP)
        grad = back + gain * ginn[STEP * b - base : STEP * b - base + STEP, :].astype(F32)
        grad = grad.astype(BF16).astype(F32)
        for i, other in ((1, 2), (2, 1)):
            value = end[other] if b == chunks else mixed_ref[other, at, lanes].astype(F32)
            gmix[i, to, :] = (grad * value).astype(BF16).astype(F32)

    skip = first_ref[0, :, lanes].astype(F32) * first_ref[1, :, lanes].astype(F32)
    for lo in range(STEP, rows, STEP):
        p = product_ref[lo : lo + STEP, lanes].astype(F32)
        skip = skip + p * inner_ref[lo : lo + STEP, lanes].astype(F32)
    sums_ref[pl.ds(64 + step, 1), :] = jnp.sum(skip, axis=0, keepdims=True)
    total = None
    for r in range(STEP):
        line = jnp.concatenate(
            [corr[half, pl.ds(r, GROUPS, stride=STEP), :] for half in (0, 1)], axis=1
        )
        line = line if r == 0 else pltpu.roll(line, 256 - r, 1)
        total = line[:, 0:128] if total is None else total + line[:, 0:128]
    sums_ref[pl.ds(pl.multiple_of(GROUPS * step, GROUPS), GROUPS), :] = total

    totals = [[None] * 7 for _ in range(3)]
    for i, known in enumerate(settled(rows)):
        stop = known + 96
        gmix[i, stop - shift : stop - shift + STEP, :] = near_gmix[i, 16:32, lanes].astype(F32)

        def store(lo, size, grad):
            grad_ref[i, lo : lo + size, :] = grad

        finish(gmix, i, stop, rows, shift, feat_ref, lanes, weights, totals[i], store)
        grad_ref[i, 0:known, :] = early_grad[i, 0:known, lanes]
        grad_ref[i, known:stop, :] = near_grad[i, :, lanes]
    lines = summed_lines(totals) + lines_ref[:, lanes]
    gather = iota((LANES, LANES), 1) == GROUPS * step + iota((LANES, LANES), 0) // 16
    gather = gather.astype(F32)
    return jnp.dot(lines, gather, precision=lax.Precision.HIGHEST, preferred_element_type=F32)


def before_kernel(*refs):
    ins, (gated_ref, *outs), scratch = refs[:14], refs[14:19], refs[19:]
    for u in range(TOGETHER):
        gated = gated_ref.at[:, LANES * u : LANES * u + LANES]
        step = TOGETHER * pl.program_id(0) + u
        before_block(step, *ins, gated, *outs, *part(scratch, u))


def after_kernel(*refs):
    ins, (grad_ref, sums_ref), scratch = refs[:15], refs[15:17], refs[17:]
    first = pl.program_id(0) == 0
    short = jnp.where(first, 0.0, sums_ref[72:96, :])
    for u in range(TOGETHER):
        grad = grad_ref.at[:, :, LANES * u : LANES * u + LANES]
        step = TOGETHER * pl.program_id(0) + u
        short = short + after_block(step, *ins, grad, sums_ref, *part(scratch, u))
    sums_ref[72:96, :] = short


def final_kernel(group_scale, token_scale, sums_ref, short_ref, long_ref, skip_ref):
    groups = long_ref.shape[0]
    values = sums_ref[...]
    long_ref[...] = values[0:groups] * group_scale
    skip_ref[...] = values[64 : 64 + skip_ref.shape[0]] * token_scale
    for i in range(3):
        short_ref[i] = values[72 + 8 * i : 79 + 8 * i, 0:groups] * group_scale


def blocks3(rows):
    return pl.BlockSpec((3, rows, TOGETHER * LANES), lambda b: (0, 0, b))


def blocks2(rows):
    return pl.BlockSpec((rows, TOGETHER * LANES), lambda b: (0, b))


def swap(values, axes):
    return lax.all_to_all(values, axes, 0, 0, tiled=True)


def summed(local):
    near, far = CTX[:2], CTX[2]
    parts = lax.axis_size(near)
    size = lax.axis_size(far)
    share = local.reshape(parts, -1, LANES)
    share = swap(share, near).sum(axis=0)
    every = jnp.broadcast_to(share[None], (size,) + share.shape)
    share = swap(every, far).sum(axis=0)
    every = jnp.broadcast_to(share[None], (parts,) + share.shape)
    return swap(every, near).reshape(local.shape)


def body(features, short_taps, long_taps, skip_gain, cotangent):
    rows, width = features.shape[1:]
    groups = width // 16
    steps = width // LANES
    inside_vmem = pl.BlockSpec(memory_space=pltpu.VMEM)
    outside = pl.BlockSpec(memory_space=pltpu.HBM)
    short_taps = short_taps.transpose(0, 2, 1)
    shape = jax.ShapeDtypeStruct

    def call(kernel, name, ins, outs, scratch, cost, grid=(), limit=LIMIT):
        return pl.pallas_call(
            kernel,
            grid=grid,
            in_specs=ins,
            out_specs=[spec for spec, _ in outs],
            out_shape=[out for _, out in outs],
            scratch_shapes=scratch,
            compiler_params=pltpu.CompilerParams(
                dimension_semantics=("arbitrary",) * len(grid), vmem_limit_bytes=limit
            ),
            cost_estimate=pl.CostEstimate(flops=cost, bytes_accessed=cost, transcendentals=0),
            name=name,
        )

    def held(*dims, dtype=BF16):
        return inside_vmem, shape(dims, dtype)

    up, down = call(
        edge_kernel,
        "edge",
        [outside] * 3,
        [(outside, shape((160, width), BF16)), (outside, shape((160, width), BF16))],
        [
            pltpu.VMEM((160, width), BF16),
            pltpu.VMEM((160, width), BF16),
            pltpu.VMEM((24, width), F32),
            pltpu.VMEM((3, 144, width), BF16),
            pltpu.VMEM((3, 144, width), BF16),
            pltpu.VMEM((144, width), BF16),
            pltpu.VMEM(short_taps.shape, BF16),
            pltpu.VMEM((AT_EDGE, 3, 152, LANES), F32),
            pltpu.SemaphoreType.DMA((steps // AT_EDGE, 8)),
            pltpu.SemaphoreType.DMA((steps // AT_EDGE, 2)),
        ],
        5 * 10**6,
        limit=EDGE_LIMIT,
    )(features, cotangent, short_taps)
    from_last = passed_along(up, CTX, 1)
    from_next = passed_along(down, CTX, -1)
    convs, backs = inside(rows)
    gain = skip_gain.reshape(steps, LANES)
    mixers = [
        held(24, width, dtype=F32),
        held(steps, LANES, dtype=F32),
        held(3, rows, width),
        held(rows, width),
        held(rows, width),
        held(groups * 16, 256),
        held(groups * 16, 256),
    ]
    sums_so_far = [held(24, width, dtype=F32), held(groups * 16, 256, dtype=F32)]
    taps, scale, *mixers_out, near_gated, near_grad, near_gmix, lines, grid = call(
        local_kernel,
        "local",
        [inside_vmem] * 5,
        mixers
        + [held(STEP * len(convs), width), held(3, 96, width), held(3, 32, width)]
        + sums_so_far,
        [
            pltpu.VMEM((AT_LOCAL, 3, rows + 8, LANES), F32),
            pltpu.VMEM((2, groups, 256), F32),
            pltpu.VMEM((AT_LOCAL, 2, 2, 128, LANES), F32),
            pltpu.VMEM((AT_LOCAL, 3, STEP * len(convs), LANES), F32),
        ],
        2 * 10**7,
    )(features, cotangent, short_taps, long_taps, gain)
    most = STEP * convs[0]
    gated, first, early_grad, *parts = call(
        before_kernel,
        "before",
        [inside_vmem] * 14,
        [
            (blocks2(rows), shape((rows, width), BF16)),
            held(2, STEP, width),
            held(3, most, width),
        ]
        + sums_so_far,
        [
            pltpu.VMEM((TOGETHER, 272, LANES), BF16),
            pltpu.VMEM((TOGETHER, WINDOW, LANES), BF16),
            pltpu.VMEM((TOGETHER, 3, most + STEP, LANES), F32),
            pltpu.VMEM((TOGETHER, 3, 24, LANES), F32),
        ],
        10**7,
        (steps // TOGETHER,),
    )(
        features, cotangent, taps, scale, *mixers_out, near_gated, near_gmix, lines, grid, from_last,
    )
    feature_grad, sums = call(
        after_kernel,
        "after",
        [inside_vmem] * 15,
        [
            (blocks3(rows), shape((3, rows, width), BF16)),
            (inside_vmem, shape((96, LANES), F32)),
        ],
        [
            pltpu.VMEM((TOGETHER, WINDOW, LANES), BF16),
            pltpu.VMEM((TOGETHER, 272, LANES), BF16),
            pltpu.VMEM((TOGETHER, 3, 160, LANES), F32),
            pltpu.VMEM((TOGETHER, 3, 24, LANES), F32),
            pltpu.VMEM((TOGETHER, 2, 128, LANES), F32),
        ],
        10**7,
        (steps // TOGETHER,),
    )(
        features, taps, scale, *mixers_out, near_grad, near_gmix, first, early_grad, *parts, from_next,
    )
    tokens = rows * lax.axis_size(CTX)
    group_scale = 1.0 / math.sqrt(16.0 * tokens)
    token_scale = 1.0 / math.sqrt(1.0 * tokens)
    short, long, skip = call(
        functools.partial(final_kernel, group_scale, token_scale),
        "final",
        [inside_vmem],
        [
            held(3, 7, groups, dtype=F32),
            held(groups, LANES, dtype=F32),
            held(steps, LANES, dtype=F32),
        ],
        [],
        10**5,
    )(summed(sums))
    return gated, feature_grad, short.transpose(0, 2, 1), long, skip.reshape(width)


def solution(mesh):
    torus = Mesh(mesh.devices.reshape(*SPLIT, mesh.shape["tp"]), CTX + ("tp",))
    return jax.shard_map(
        body,
        mesh=torus,
        in_specs=(P(None, CTX, "tp"), P(None, "tp", None), P("tp", None), P("tp"), P(CTX, "tp")),
        out_specs=(P(CTX, "tp"), P(None, CTX, "tp"), P(None, "tp", None), P("tp", None), P("tp")),
        check_vma=False,
    )
```

```python
import functools
import math

import jax
import jax.numpy as jnp
from jax import lax
from jax.experimental import pallas as pl
from jax.experimental.pallas import tpu as pltpu
from jax.sharding import Mesh
from jax.sharding import PartitionSpec as P

CTX = ("ctx_0", "ctx_1", "ctx_2")
SPLIT = (4, 3, 8)
LANES = 128
GROUPS = 8
STEP = 16
WINDOW = 144
BF16 = jnp.bfloat16
F32 = jnp.float32
LIMIT = 16 * 2**20
TOGETHER, AT_EDGE, AT_LOCAL = 4, 4, 1
LAG_LOCAL, LAG_BEFORE, LAG_AFTER = 1000, 4, 8
EDGE_LIMIT = 60000 * 2**10


def passed_along(block, axis, distance):
    devices = range(lax.axis_size(axis))
    route = [(i - distance, i) for i in devices if i - distance in devices]
    return lax.ppermute(block, axis, route)


def iota(shape, dim):
    return lax.broadcasted_iota(jnp.int32, shape, dim)


def lanes_of(step):
    if isinstance(step, int):
        return pl.ds(LANES * step, LANES)
    return pl.ds(pl.multiple_of(LANES * step, LANES), LANES)


def channel_taps(taps_ref, out_ref):
    shape = (taps_ref.shape[2], out_ref.shape[1])
    spread = iota(shape, 0) == iota(shape, 1) // 16
    spread = spread.astype(F32).astype(BF16)
    for i in range(3):
        out_ref[8 * i : 8 * i + 7, :] = jnp.dot(
            taps_ref[i], spread, preferred_element_type=F32
        )


def staggered(blocks, lag):
    waiting, running, results = list(enumerate(blocks)), [], [None] * len(blocks)
    stage = 0
    while waiting or running:
        if waiting and (stage % lag == 0 or not running):
            running.append(waiting.pop(0))
        for item in list(running):
            try:
                next(item[1])
            except StopIteration as stop:
                results[item[0]] = stop.value
                running.remove(item)
        stage += 1
    return results


def part(refs, u):
    return [ref.at[u] for ref in refs]


def causal(ref, i, start, rows, taps):
    total = None
    for j in range(7):
        term = taps[8 * i + j : 8 * i + j + 1, :] * ref[i, start - j : start - j + rows, :]
        total = term if total is None else total + term
    return total.astype(BF16)


def pick_groups(full, masks):
    total = full[0:STEP]
    for g in range(1, GROUPS):
        total = jnp.where(masks[g], full[STEP * g : STEP * g + STEP], total)
    return total


def group_masks():
    group_of = iota((STEP, LANES), 1) // 16
    return [group_of == g for g in range(GROUPS)]


def filtered(matrix, ref, shift, chunks, masks, lanes):
    for at in range(0, len(chunks), 2):
        own = chunks[at : at + 2]
        parts = [ref[STEP * b + shift : STEP * b + shift + WINDOW, lanes] for b in own]
        parts = parts[0] if len(parts) == 1 else jnp.concatenate(parts, axis=1)
        full = jnp.dot(matrix, parts, preferred_element_type=F32)
        for n, b in enumerate(own):
            yield b, pick_groups(full[:, LANES * n : LANES * n + LANES], masks)


def inside(rows):
    chunks = rows // STEP
    return list(range(9, chunks)), list(range(1, chunks - 8))


def correlated(grid, products, inners, chunks, keep):
    for at in range(0, len(chunks), 2):
        own = chunks[at : at + 2]
        pieces = [products(b) for b in own]
        windows = [inners(b) for b in own]
        right = windows[0] if len(own) == 1 else jnp.concatenate(windows, axis=1)
        left = []
        for k in keep:
            masked = [k * p for p in pieces]
            left.append(masked[0] if len(own) == 1 else jnp.concatenate(masked, axis=1))
        term = lax.dot_general(
            jnp.concatenate(left, axis=0), right, (((1,), (1,)), ((), ())),
            preferred_element_type=F32,
        )
        grid = term if grid is None else grid + term
    return grid


def short_pass(gmix, i, own, weights, totals, lo, size):
    grad = None
    for j in range(7):
        moved = gmix[i, lo + j : lo + j + size, :]
        term = weights[8 * i + j : 8 * i + j + 1, :] * moved
        grad = term if grad is None else grad + term
        both = (moved * own).reshape(size // 8, 8, LANES).sum(axis=0)
        totals[j] = both if totals[j] is None else totals[j] + both
    return grad.astype(BF16)


def settled(rows):
    return [rows - 112, 16, 16]


def edge_kernel(
    feat_hbm, cot_hbm, taps_hbm, up_hbm, down_hbm,
    up_ref, down_ref, taps, opens, closes, cot_ref, taps_ref, raws, sems, out_sems,
):
    rows, width = cot_hbm.shape
    span = AT_EDGE * LANES

    def block(step, raw):
        lanes = lanes_of(step)
        weights = taps[:, lanes]
        raw[0, 0:8, :] = jnp.zeros((8, LANES), F32)
        raw[0, 8:152, :] = opens[0, :, lanes].astype(F32)
        for i in (1, 2):
            raw[i, 0:144, :] = closes[i, :, lanes].astype(F32)
        for lo in (0, 64):
            key = causal(raw, 1, 16 + lo, 64, weights).astype(F32)
            value = causal(raw, 2, 16 + lo, 64, weights).astype(F32)
            up_ref[lo : lo + 64, lanes] = (key * value).astype(BF16)
        last = [closes[i, 128:144, lanes].astype(F32)[8:16] for i in range(3)]
        blank = jnp.zeros((8, LANES), F32)
        up_ref[128:160, lanes] = jnp.concatenate(last + [blank], axis=0).astype(BF16)
        for lo in (0, 64):
            inner = causal(raw, 0, 8 + lo, 64, weights).astype(F32)
            grad = cot_ref[lo : lo + 64, lanes].astype(F32)
            inner = grad * inner
            if lo == 0:
                first = jnp.where(iota((8, LANES), 0) < 6, grad[0:8], inner[0:8])
                inner = jnp.concatenate([first, inner[8:64]], axis=0)
            down_ref[lo : lo + 64, lanes] = inner.astype(BF16)
        query = causal(raw, 0, 136, 8, weights).astype(F32)
        rest = cot_ref[128:144, lanes].astype(F32)[0:8] * query
        begin = [opens[i, 0:16, lanes].astype(F32)[0:8] for i in range(3)]
        down_ref[128:160, lanes] = jnp.concatenate([rest] + begin, axis=0).astype(BF16)

    def fetches(at):
        lanes = pl.ds(span * at, span)
        pairs = [
            (feat_hbm.at[1, rows - 144 : rows, lanes], closes.at[1, :, lanes]),
            (feat_hbm.at[2, rows - 144 : rows, lanes], closes.at[2, :, lanes]),
            (feat_hbm.at[0, 0:144, lanes], opens.at[0, :, lanes]),
            (cot_hbm.at[0:144, lanes], cot_ref.at[:, lanes]),
            (feat_hbm.at[0, rows - 16 : rows, lanes], closes.at[0, 128:144, lanes]),
            (feat_hbm.at[1, 0:16, lanes], opens.at[1, 0:16, lanes]),
            (feat_hbm.at[2, 0:16, lanes], opens.at[2, 0:16, lanes]),
        ]
        return [
            pltpu.make_async_copy(source, target, sems.at[at, n])
            for n, (source, target) in enumerate(pairs)
        ]

    def stores(at):
        lanes = pl.ds(span * at, span)
        return [
            pltpu.make_async_copy(up_ref.at[:, lanes], up_hbm.at[:, lanes], out_sems.at[at, 0]),
            pltpu.make_async_copy(
                down_ref.at[:, lanes], down_hbm.at[:, lanes], out_sems.at[at, 1]
            ),
        ]

    turns = range(width // span)
    first = pltpu.make_async_copy(taps_hbm, taps_ref, sems.at[0, 7])
    first.start()
    for at in turns:
        for copy in fetches(at):
            copy.start()
    first.wait()
    channel_taps(taps_ref, taps)
    for at in turns:
        for copy in fetches(at):
            copy.wait()
        for u in range(AT_EDGE):
            block(AT_EDGE * at + u, raws.at[u])
        for copy in stores(at):
            copy.start()
    for at in turns:
        for copy in stores(at):
            copy.wait()


def local_kernel(
    feat_ref, cot_ref, taps_ref, long_ref, gain_ref,
    taps_out, gain_out, mixed_ref, product_ref, inner_ref, ahead_ref, behind_ref,
    gated_ref, grad_ref, gmix_ref, lines_ref, grid_ref,
    raws, filt, spreads, gmixes,
):
    rows = cot_ref.shape[0]
    groups = long_ref.shape[0]
    flip = iota((128, 256), 0) + iota((128, 256), 1) == 128
    flip = flip.astype(F32).astype(BF16)
    filt[0] = jnp.dot(long_ref[...], flip, preferred_element_type=F32)
    filt[1, :, 0:128] = long_ref[...].astype(F32)
    filt[1, :, 128:256] = jnp.zeros((groups, 128), F32)

    channel_taps(taps_ref, taps_out)
    gain_out[...] = gain_ref[...].astype(F32)

    def one(step, raw, spread, gmix):
        lanes = lanes_of(step)
        block = pl.ds(pl.multiple_of(LANES * step, LANES), LANES)
        gain = gain_out[pl.ds(step, 1), :]
        weights = taps_out[:, lanes]
        for which, out in ((0, ahead_ref), (1, behind_ref)):
            base = filt[which, pl.ds(pl.multiple_of(GROUPS * step, GROUPS), GROUPS), :]
            for r in range(STEP):
                moved = base if r == 0 else pltpu.roll(base, r, 1)
                for half in (0, 1):
                    part = moved[:, 128 * half : 128 * half + 128]
                    spread[which, half, pl.ds(r, GROUPS, stride=STEP), :] = part
            for half in (0, 1):
                out[block, 128 * half : 128 * half + 128] = spread[which, half].astype(BF16)
            yield
        for i in range(3):
            raw[i, 0:8, :] = jnp.zeros((8, LANES), F32)
            raw[i, 8 : 8 + rows, :] = feat_ref[i, :, lanes].astype(F32)
        size = 64
        for lo in range(0, rows, size):
            query, key, value = [causal(raw, i, 8 + lo, size, weights) for i in range(3)]
            mixed_ref[0, lo : lo + size, lanes] = query
            mixed_ref[1, lo : lo + size, lanes] = key
            mixed_ref[2, lo : lo + size, lanes] = value
            both = key.astype(F32) * value.astype(F32)
            product_ref[lo : lo + size, lanes] = both.astype(BF16)
            grad = cot_ref[lo : lo + size, lanes].astype(F32)
            inner_ref[lo : lo + size, lanes] = (grad * query.astype(F32)).astype(BF16)
            yield
        masks = group_masks()
        keep = [m.astype(F32).astype(BF16) for m in masks]
        convs, backs = inside(rows)
        starts = settled(rows)
        matrix = ahead_ref[block, 0:WINDOW]
        for b, conv in filtered(matrix, product_ref, -128, convs, masks, lanes):
            at = slice(STEP * b, STEP * b + STEP)
            to = slice(STEP * (b - convs[0]), STEP * (b - convs[0]) + STEP)
            inner = conv + gain * product_ref[at, lanes].astype(F32)
            grad = (cot_ref[at, lanes].astype(F32) * inner).astype(BF16)
            gmix[0, to, :] = grad.astype(F32)
            gated_ref[to, lanes] = (mixed_ref[0, at, lanes].astype(F32) * inner).astype(BF16)
            if b == convs[0] or b == convs[-1]:
                half = STEP * (b == convs[-1])
                gmix_ref[0, half : half + STEP, lanes] = grad
            yield
        matrix = behind_ref[block, 0:WINDOW]
        for b, back in filtered(matrix, inner_ref, 0, backs, masks, lanes):
            at = slice(STEP * b, STEP * b + STEP)
            to = slice(STEP * (b - backs[0]), STEP * (b - backs[0]) + STEP)
            grad = back + gain * inner_ref[at, lanes].astype(F32)
            grad = grad.astype(BF16).astype(F32)
            for i, other in ((1, 2), (2, 1)):
                value = (grad * mixed_ref[other, at, lanes].astype(F32)).astype(BF16)
                gmix[i, to, :] = value.astype(F32)
                if b == backs[0] or b == backs[-1]:
                    half = STEP * (b == backs[-1])
                    gmix_ref[i, half : half + STEP, lanes] = value
            yield
        for i in range(3):
            totals = [None] * 7
            for lo in (0, 48):
                at = starts[i] + lo
                own = feat_ref[i, at : at + 48, lanes].astype(F32)
                grad_ref[i, lo : lo + 48, lanes] = short_pass(
                    gmix, i, own, weights, totals, lo, 48
                )
                yield
            lines = [jnp.sum(total, axis=0, keepdims=True) for total in totals]
            lines.append(jnp.zeros((1, LANES), F32))
            lines_ref[8 * i : 8 * i + 8, lanes] = jnp.concatenate(lines, axis=0)
        grid_ref[block, 0:WINDOW] = correlated(
            None,
            lambda b: product_ref[STEP * b : STEP * b + STEP, lanes],
            lambda b: inner_ref[STEP * b : STEP * b + WINDOW, lanes],
            backs,
            keep,
        )

    @pl.loop(0, cot_ref.shape[1] // LANES // AT_LOCAL)
    def _(step):
        staggered(
            [
                one(AT_LOCAL * step + u, *part((raws, spreads, gmixes), u))
                for u in range(AT_LOCAL)
            ],
            LAG_LOCAL,
        )


def finish(gmix, i, low, high, shift, feat_ref, lanes, weights, totals, store):
    for lo in range(low, high, 48):
        size = min(48, high - lo)
        own = feat_ref[i, lo : lo + size, lanes].astype(F32)
        store(lo, size, short_pass(gmix, i, own, weights, totals, lo - shift, size))
        yield


def summed_lines(totals):
    lines = []
    for parts in totals:
        lines += [jnp.sum(part, axis=0, keepdims=True) for part in parts]
        lines.append(jnp.zeros((1, LANES), F32))
    return jnp.concatenate(lines, axis=0)


def before_block(
    step, feat_ref, cot_ref, taps_ref, gain_ref, mixed_ref, product_ref, inner_ref, ahead_ref, behind_ref,
    near_gated, near_gmix, lines_ref, grid_ref, up_ref,
    gated_ref, first_ref, grad_ref, lines_out, grid_out,
    prod, ginn, gmix, raw,
):
    rows = cot_ref.shape[0]
    lanes = lanes_of(step)
    block = pl.ds(pl.multiple_of(LANES * step, LANES), LANES)
    every = pl.ds(0, LANES)
    weights = taps_ref[:, lanes]
    gain = gain_ref[pl.ds(step, 1), :]
    masks = group_masks()
    keep = [m.astype(F32).astype(BF16) for m in masks]
    convs, backs = inside(rows)

    before = up_ref[128:160, lanes].astype(F32)
    start = []
    for i in range(3):
        raw[i, 0:8, :] = before[8 * i : 8 * i + 8]
        raw[i, 8:24, :] = feat_ref[i, 0:16, lanes].astype(F32)
        first = causal(raw, i, 8, 8, weights).astype(F32)
        second = mixed_ref[i, 0:16, lanes].astype(F32)[8:16]
        start.append(jnp.concatenate([first, second], axis=0))
    product = (start[1] * start[2]).astype(BF16)
    inners = (cot_ref[0:16, lanes].astype(F32) * start[0]).astype(BF16)
    first_ref[0, :, lanes] = product
    first_ref[1, :, lanes] = inners
    prod[0:128, :] = up_ref[0:128, lanes]
    prod[128:144, :] = product
    prod[144:272, :] = product_ref[16:144, lanes]
    ginn[0:16, :] = inners
    ginn[16:144, :] = inner_ref[16:144, lanes]

    grid_out[block, 0:WINDOW] = correlated(
        grid_ref[block, 0:WINDOW], lambda b: product, lambda b: ginn[...], [0], keep
    )
    yield
    outer = list(range(convs[0]))
    for b, conv in filtered(ahead_ref[block, 0:WINDOW], prod, 0, outer, masks, every):
        at = slice(STEP * b, STEP * b + STEP)
        inner = conv + gain * prod[128 + STEP * b : 144 + STEP * b, :].astype(F32)
        query = start[0] if b == 0 else mixed_ref[0, at, lanes].astype(F32)
        gmix[0, at, :] = (cot_ref[at, lanes].astype(F32) * inner).astype(BF16).astype(F32)
        gated_ref[at, :] = (query * inner).astype(BF16)
        yield
    gated_ref[STEP * convs[0] : rows, :] = near_gated[:, lanes]
    for b, back in filtered(behind_ref[block, 0:WINDOW], ginn, 0, [0], masks, every):
        grad = back + gain * inners.astype(F32)
        grad = grad.astype(BF16).astype(F32)
        gmix[1, 0:16, :] = (grad * start[2]).astype(BF16).astype(F32)
        gmix[2, 0:16, :] = (grad * start[1]).astype(BF16).astype(F32)
    totals = [[None] * 7 for _ in range(3)]
    for i, known in enumerate(settled(rows)):
        gmix[i, known : known + 16, :] = near_gmix[i, 0:16, lanes].astype(F32)

        def store(lo, size, grad):
            grad_ref[i, lo : lo + size, lanes] = grad

        yield from finish(gmix, i, 0, known, 0, feat_ref, lanes, weights, totals[i], store)
    lines_out[:, lanes] = lines_ref[:, lanes] + summed_lines(totals)


def after_block(
    step, feat_ref, taps_ref, gain_ref, mixed_ref, product_ref, inner_ref, ahead_ref, behind_ref,
    near_grad, near_gmix, first_ref, early_grad, lines_ref, grid_ref, down_ref,
    grad_ref, sums_ref,
    prod, ginn, gmix, raw, corr,
):
    rows = feat_ref.shape[1]
    chunks = rows // STEP
    lanes = lanes_of(step)
    block = pl.ds(pl.multiple_of(LANES * step, LANES), LANES)
    every = pl.ds(0, LANES)
    weights = taps_ref[:, lanes]
    gain = gain_ref[pl.ds(step, 1), :]
    masks = group_masks()
    keep = [m.astype(F32).astype(BF16) for m in masks]
    convs, backs = inside(rows)
    base = rows - 128

    tail = down_ref[128:160, lanes].astype(F32)
    end = []
    for i in range(3):
        raw[i, 0:16, :] = feat_ref[i, rows - 16 : rows, lanes].astype(F32)
        raw[i, 16:24, :] = tail[8 + 8 * i : 16 + 8 * i]
        past_end = causal(raw, i, 16, 8, weights).astype(F32)
        end.append(jnp.concatenate([past_end, jnp.zeros((8, LANES), F32)], axis=0))
    opening = down_ref[0:16, lanes].astype(F32)
    past = iota((STEP, LANES), 0) < 6
    after = jnp.where(past, opening, 0.0)
    prod[0:128, :] = product_ref[base:rows, lanes]
    prod[128:144, :] = (end[1] * end[2]).astype(BF16)
    ginn[0:128, :] = inner_ref[base:rows, lanes]
    ginn[128:144, :] = jnp.where(past, after * end[0], opening).astype(BF16)
    ginn[144:256, :] = down_ref[16:128, lanes]
    ginn[256:272, :] = jnp.concatenate(
        [tail[0:8], jnp.zeros((8, LANES), F32)], axis=0
    ).astype(BF16)

    outer = list(range(backs[-1] + 1, chunks))
    yield
    grid = grid_ref[block, 0:WINDOW]
    for at in range(0, len(outer), 2):
        grid = correlated(
            grid,
            lambda b: prod[STEP * b - base : STEP * b - base + STEP, :],
            lambda b: ginn[STEP * b - base : STEP * b - base + WINDOW, :],
            outer[at : at + 2],
            keep,
        )
        yield
    corr[0] = grid[:, 0:128]
    corr[1, :, 0 : WINDOW - 128] = grid[:, 128:WINDOW]
    corr[1, :, WINDOW - 128 : 128] = jnp.zeros((LANES, 256 - WINDOW), F32)

    shift = base - STEP
    for b, conv in filtered(ahead_ref[block, 0:WINDOW], prod, -base - 128, [chunks], masks, every):
        inner = conv + gain * prod[128:144, :].astype(F32)
        gmix[0, rows - shift : rows - shift + STEP, :] = (after * inner).astype(BF16).astype(F32)
    outer.append(chunks)
    for b, back in filtered(behind_ref[block, 0:WINDOW], ginn, -base, outer, masks, every):
        at = slice(STEP * b, STEP * b + STEP)
        to = slice(STEP * b - shift, STEP * b - shift + STEP)
        grad = back + gain * ginn[STEP * b - base : STEP * b - base + STEP, :].astype(F32)
        grad = grad.astype(BF16).astype(F32)
        for i, other in ((1, 2), (2, 1)):
            value = end[other] if b == chunks else mixed_ref[other, at, lanes].astype(F32)
            gmix[i, to, :] = (grad * value).astype(BF16).astype(F32)
        yield

    skip = first_ref[0, :, lanes].astype(F32) * first_ref[1, :, lanes].astype(F32)
    for lo in range(STEP, rows, STEP):
        p = product_ref[lo : lo + STEP, lanes].astype(F32)
        skip = skip + p * inner_ref[lo : lo + STEP, lanes].astype(F32)
    sums_ref[pl.ds(64 + step, 1), :] = jnp.sum(skip, axis=0, keepdims=True)
    total = None
    for r in range(STEP):
        line = jnp.concatenate(
            [corr[half, pl.ds(r, GROUPS, stride=STEP), :] for half in (0, 1)], axis=1
        )
        line = line if r == 0 else pltpu.roll(line, 256 - r, 1)
        total = line[:, 0:128] if total is None else total + line[:, 0:128]
    sums_ref[pl.ds(pl.multiple_of(GROUPS * step, GROUPS), GROUPS), :] = total

    totals = [[None] * 7 for _ in range(3)]
    for i, known in enumerate(settled(rows)):
        stop = known + 96
        gmix[i, stop - shift : stop - shift + STEP, :] = near_gmix[i, 16:32, lanes].astype(F32)

        def store(lo, size, grad):
            grad_ref[i, lo : lo + size, :] = grad

        yield from finish(gmix, i, stop, rows, shift, feat_ref, lanes, weights, totals[i], store)
        grad_ref[i, 0:known, :] = early_grad[i, 0:known, lanes]
        grad_ref[i, known:stop, :] = near_grad[i, :, lanes]
    lines = summed_lines(totals) + lines_ref[:, lanes]
    gather = iota((LANES, LANES), 1) == GROUPS * step + iota((LANES, LANES), 0) // 16
    gather = gather.astype(F32)
    return jnp.dot(lines, gather, precision=lax.Precision.HIGHEST, preferred_element_type=F32)


def before_kernel(*refs):
    ins, (gated_ref, *outs), scratch = refs[:14], refs[14:19], refs[19:]
    blocks = []
    for u in range(TOGETHER):
        gated = gated_ref.at[:, LANES * u : LANES * u + LANES]
        step = TOGETHER * pl.program_id(0) + u
        blocks.append(before_block(step, *ins, gated, *outs, *part(scratch, u)))
    staggered(blocks, LAG_BEFORE)


def after_kernel(*refs):
    ins, (grad_ref, sums_ref), scratch = refs[:15], refs[15:17], refs[17:]
    first = pl.program_id(0) == 0
    short = jnp.where(first, 0.0, sums_ref[72:96, :])
    blocks = []
    for u in range(TOGETHER):
        grad = grad_ref.at[:, :, LANES * u : LANES * u + LANES]
        step = TOGETHER * pl.program_id(0) + u
        blocks.append(after_block(step, *ins, grad, sums_ref, *part(scratch, u)))
    for term in staggered(blocks, LAG_AFTER):
        short = short + term
    sums_ref[72:96, :] = short


def final_kernel(group_scale, token_scale, sums_ref, short_ref, long_ref, skip_ref):
    groups = long_ref.shape[0]
    values = sums_ref[...]
    long_ref[...] = values[0:groups] * group_scale
    skip_ref[...] = values[64 : 64 + skip_ref.shape[0]] * token_scale
    for i in range(3):
        short_ref[i] = values[72 + 8 * i : 79 + 8 * i, 0:groups] * group_scale


def blocks3(rows):
    return pl.BlockSpec((3, rows, TOGETHER * LANES), lambda b: (0, 0, b))


def blocks2(rows):
    return pl.BlockSpec((rows, TOGETHER * LANES), lambda b: (0, b))


def swap(values, axes):
    return lax.all_to_all(values, axes, 0, 0, tiled=True)


def summed(local):
    near, far = CTX[:2], CTX[2]
    parts = lax.axis_size(near)
    size = lax.axis_size(far)
    share = local.reshape(parts, -1, LANES)
    share = swap(share, near).sum(axis=0)
    every = jnp.broadcast_to(share[None], (size,) + share.shape)
    share = swap(every, far).sum(axis=0)
    every = jnp.broadcast_to(share[None], (parts,) + share.shape)
    return swap(every, near).reshape(local.shape)


def body(features, short_taps, long_taps, skip_gain, cotangent):
    rows, width = features.shape[1:]
    groups = width // 16
    steps = width // LANES
    inside_vmem = pl.BlockSpec(memory_space=pltpu.VMEM)
    outside = pl.BlockSpec(memory_space=pltpu.HBM)
    short_taps = short_taps.transpose(0, 2, 1)
    shape = jax.ShapeDtypeStruct

    def call(kernel, name, ins, outs, scratch, cost, grid=(), limit=LIMIT):
        return pl.pallas_call(
            kernel,
            grid=grid,
            in_specs=ins,
            out_specs=[spec for spec, _ in outs],
            out_shape=[out for _, out in outs],
            scratch_shapes=scratch,
            compiler_params=pltpu.CompilerParams(
                dimension_semantics=("arbitrary",) * len(grid), vmem_limit_bytes=limit
            ),
            cost_estimate=pl.CostEstimate(flops=cost, bytes_accessed=cost, transcendentals=0),
            name=name,
        )

    def held(*dims, dtype=BF16):
        return inside_vmem, shape(dims, dtype)

    up, down = call(
        edge_kernel,
        "edge",
        [outside] * 3,
        [(outside, shape((160, width), BF16)), (outside, shape((160, width), BF16))],
        [
            pltpu.VMEM((160, width), BF16),
            pltpu.VMEM((160, width), BF16),
            pltpu.VMEM((24, width), F32),
            pltpu.VMEM((3, 144, width), BF16),
            pltpu.VMEM((3, 144, width), BF16),
            pltpu.VMEM((144, width), BF16),
            pltpu.VMEM(short_taps.shape, BF16),
            pltpu.VMEM((AT_EDGE, 3, 152, LANES), F32),
            pltpu.SemaphoreType.DMA((steps // AT_EDGE, 8)),
            pltpu.SemaphoreType.DMA((steps // AT_EDGE, 2)),
        ],
        5 * 10**6,
        limit=EDGE_LIMIT,
    )(features, cotangent, short_taps)
    from_last = passed_along(up, CTX, 1)
    from_next = passed_along(down, CTX, -1)
    convs, backs = inside(rows)
    gain = skip_gain.reshape(steps, LANES)
    mixers = [
        held(24, width, dtype=F32),
        held(steps, LANES, dtype=F32),
        held(3, rows, width),
        held(rows, width),
        held(rows, width),
        held(groups * 16, 256),
        held(groups * 16, 256),
    ]
    sums_so_far = [held(24, width, dtype=F32), held(groups * 16, 256, dtype=F32)]
    taps, scale, *mixers_out, near_gated, near_grad, near_gmix, lines, grid = call(
        local_kernel,
        "local",
        [inside_vmem] * 5,
        mixers
        + [held(STEP * len(convs), width), held(3, 96, width), held(3, 32, width)]
        + sums_so_far,
        [
            pltpu.VMEM((AT_LOCAL, 3, rows + 8, LANES), F32),
            pltpu.VMEM((2, groups, 256), F32),
            pltpu.VMEM((AT_LOCAL, 2, 2, 128, LANES), F32),
            pltpu.VMEM((AT_LOCAL, 3, STEP * len(convs), LANES), F32),
        ],
        2 * 10**7,
    )(features, cotangent, short_taps, long_taps, gain)
    most = STEP * convs[0]
    gated, first, early_grad, *parts = call(
        before_kernel,
        "before",
        [inside_vmem] * 14,
        [
            (blocks2(rows), shape((rows, width), BF16)),
            held(2, STEP, width),
            held(3, most, width),
        ]
        + sums_so_far,
        [
            pltpu.VMEM((TOGETHER, 272, LANES), BF16),
            pltpu.VMEM((TOGETHER, WINDOW, LANES), BF16),
            pltpu.VMEM((TOGETHER, 3, most + STEP, LANES), F32),
            pltpu.VMEM((TOGETHER, 3, 24, LANES), F32),
        ],
        10**7,
        (steps // TOGETHER,),
    )(
        features, cotangent, taps, scale, *mixers_out, near_gated, near_gmix, lines, grid, from_last,
    )
    feature_grad, sums = call(
        after_kernel,
        "after",
        [inside_vmem] * 15,
        [
            (blocks3(rows), shape((3, rows, width), BF16)),
            (inside_vmem, shape((96, LANES), F32)),
        ],
        [
            pltpu.VMEM((TOGETHER, WINDOW, LANES), BF16),
            pltpu.VMEM((TOGETHER, 272, LANES), BF16),
            pltpu.VMEM((TOGETHER, 3, 160, LANES), F32),
            pltpu.VMEM((TOGETHER, 3, 24, LANES), F32),
            pltpu.VMEM((TOGETHER, 2, 128, LANES), F32),
        ],
        10**7,
        (steps // TOGETHER,),
    )(
        features, taps, scale, *mixers_out, near_grad, near_gmix, first, early_grad, *parts, from_next,
    )
    tokens = rows * lax.axis_size(CTX)
    group_scale = 1.0 / math.sqrt(16.0 * tokens)
    token_scale = 1.0 / math.sqrt(1.0 * tokens)
    short, long, skip = call(
        functools.partial(final_kernel, group_scale, token_scale),
        "final",
        [inside_vmem],
        [
            held(3, 7, groups, dtype=F32),
            held(groups, LANES, dtype=F32),
            held(steps, LANES, dtype=F32),
        ],
        [],
        10**5,
    )(summed(sums))
    return gated, feature_grad, short.transpose(0, 2, 1), long, skip.reshape(width)


def solution(mesh):
    torus = Mesh(mesh.devices.reshape(*SPLIT, mesh.shape["tp"]), CTX + ("tp",))
    return jax.shard_map(
        body,
        mesh=torus,
        in_specs=(P(None, CTX, "tp"), P(None, "tp", None), P("tp", None), P("tp"), P(CTX, "tp")),
        out_specs=(P(CTX, "tp"), P(None, CTX, "tp"), P(None, "tp", None), P("tp", None), P("tp")),
        check_vma=False,
    )
```
